256 devices in a mesh: lat: 64 (over x, y_hi, z), lon: 4 (over y_lo, core).
Axes of the slice: x: 4, y: 4 (y_hi: 2, y_lo: 2; y = y_hi * 2 + y_lo), z: 8, core: 2. Of those that a mesh axis runs over, the one named last changes fastest.
Arguments:
- tracer: float32 [32, 1536, 1152], P(None, 'lat', 'lon'), may hold values from -6 to 6
- wind_u: float32 [32, 1536, 1152], P(None, 'lat', 'lon'), may hold values from -2.5 to 2.5
- wind_v: float32 [32, 1536, 1152], P(None, 'lat', 'lon'), may hold values from -2.5 to 2.5
- ocean_temp: float32 [4, 2048, 3584], P(None, 'lat', 'lon'), may hold values from -6 to 6
- land_mask: int32 [2048, 3584], P('lat', 'lon'), may hold values 0 or 1
- remap_rows: int32 [2048, 3584], P('lat', 'lon'), may hold values from 0 to 1535, as said below
- remap_cols: int32 [2048, 3584], P('lat', 'lon'), may hold values from 0 to 1151, as said below
- polar_rows: int32 [192], replicated, may hold values from 0 to 1535, as said below
Outputs:
- tracer_out: float32 [32, 1536, 1152], P(None, 'lat', 'lon')
- ocean_out: float32 [4, 2048, 3584], P(None, 'lat', 'lon')
The draws below stay inside these ranges and needn't reach their ends.
Inputs may be any that keep to these rules, and one draw needn't show every extreme that they name: `remap_rows`: for an ocean cell in row block b of 32 rows, an atmosphere row from b * 24 - 1 to (b + 1) * 24, within the grid. `remap_cols`: for an ocean cell in column block c of 896 columns, an atmosphere column from c * 288 - 1 to (c + 1) * 288, modulo 1152. `polar_rows`: distinct rows, each among the 192 rows nearest either pole.
All inputs are finite; a program needn't handle non-finite values. No bound on the sum of `land_mask` on one device may be relied on, other than what follows from the above.
Results may differ from the reference program's by a relative error of at most 0.0001.
Values sent between devices are 32-bit elements; how exact they have to be, the bound alone decides.
No kernel may reach another device: no remote copies, remote signals or barrier semaphores. Data moves between devices by JAX's collectives and lax.ppermute only.
A program may use at most 128 MiB of HBM per device.

```python
import math
import jax
import jax.numpy as jnp

NLON = 1152
ROWS = 24
LEV = 32
STEPS = 2
OSTEPS = 2
OLEV = 4
OROWS = 32
OCOLS = 896
NLAT = 1536
LON_DEV = 288
BAND = 192
ONY = 2048
ONX = 3584


def draw_remap_rows(key, part):
    base_row = jnp.arange(ONY, dtype=jnp.int32)[:, None] // OROWS * ROWS - 1
    offset = jax.random.randint(key, (ONY, ONX), 0, ROWS + 2)
    return jnp.clip(base_row + offset, 0, NLAT - 1).astype(jnp.int32)


def draw_remap_cols(key, part):
    base_col = jnp.arange(ONX, dtype=jnp.int32)[None, :] // OCOLS * LON_DEV - 1
    offset = jax.random.randint(key, (ONY, ONX), 0, LON_DEV + 2)
    return ((base_col + offset) % NLON).astype(jnp.int32)


def draw_polar_rows(key, part):
    band_index = jnp.arange(2 * BAND, dtype=jnp.int32)
    band_row = jnp.where(band_index < BAND, band_index, NLAT - 2 * BAND + band_index)
    order = jax.random.permutation(key, 2 * BAND)
    return band_row[order[:BAND]].astype(jnp.int32)


def place_ends(array, stream_key, smallest, top_value):
    spot = [jax.random.randint(jax.random.fold_in(stream_key, axis), (), 0, length) for axis, length in enumerate(array.shape)]
    widest = array.shape.index(max(array.shape))
    beside = spot[:widest] + [(spot[widest] + 1) % array.shape[widest]] + spot[widest + 1:]
    return array.at[tuple(spot)].set(smallest).at[tuple(beside)].set(top_value)


def block_scale(key, extent, pieces, low, top_value):
    def one(axis_at, parts):
        heights = jax.random.uniform(jax.random.fold_in(jax.random.fold_in(key, 6), axis_at), (parts,), jnp.float32, low / len(pieces), top_value / len(pieces))
        return jnp.repeat(jnp.exp(heights), extent[axis_at] // parts).reshape((-1,) + (1,) * (len(extent) - axis_at - 1))

    factor_of = one(*pieces[0])
    for cut in pieces[1:]:
        factor_of = factor_of * one(*cut)
    return factor_of


def bell_draw(key, shape, deviation, most, split=(), kind=jnp.bfloat16):
    array = jax.random.normal(key, shape, jnp.float32) * deviation
    if len(split) > 0:
        array = block_scale(key, shape, split, -0.22, 0.18) * array
    return jnp.clip(array, min=-most, max=most).astype(kind)


def setup_inputs(seed: int = 0) -> dict:
    arg_keys = jax.random.split(jax.random.key(seed), 9)
    tracer = bell_draw(arg_keys[0], (LEV, NLAT, NLON), 1.0, 6.0, ((1, 64), (2, 4)), jnp.float32)
    wind_u = bell_draw(arg_keys[1], (LEV, NLAT, NLON), 0.4, 2.5, ((1, 64), (2, 4)), jnp.float32)
    wind_v = bell_draw(arg_keys[2], (LEV, NLAT, NLON), 0.4, 2.5, ((1, 64), (2, 4)), jnp.float32)
    ocean_temp = bell_draw(arg_keys[3], (OLEV, ONY, ONX), 1.0, 6.0, ((1, 64), (2, 4)), jnp.float32)
    land_mask = place_ends((jax.random.randint(arg_keys[4], (ONY, ONX), 0, 10) < 7).astype(jnp.int32), jax.random.fold_in(arg_keys[4], 1), 0, 1)
    remap_rows = draw_remap_rows(jax.random.fold_in(arg_keys[8], 71), 0)
    remap_cols = draw_remap_cols(jax.random.fold_in(arg_keys[8], 71), 0)
    polar_rows = draw_polar_rows(jax.random.fold_in(arg_keys[8], 71), 0)
    return dict(tracer=tracer, wind_u=wind_u, wind_v=wind_v, ocean_temp=ocean_temp, land_mask=land_mask, remap_rows=remap_rows, remap_cols=remap_cols, polar_rows=polar_rows)


advect_coef = 0.2
diffuse_coef = 0.1
flux_coef = 0.25
ocean_diffuse = 0.15
vertical_mix = 0.2


def damp_table(row_index, polar_rows, wave_numbers):
    latitude_cos = jnp.sin(math.pi * (row_index.astype(jnp.float32) + 0.5) / NLAT)
    ratio = latitude_cos / math.sin(math.pi * BAND / NLAT)
    wave_sine = jnp.sin(math.pi * wave_numbers / NLON)
    safe_sine = jnp.where(wave_numbers > 0.5, wave_sine, 1.0)
    damping = jnp.where(wave_numbers[None, :] > 0.5, jnp.minimum(1.0, ratio[:, None] / safe_sine[None, :]), 1.0)
    listed = jnp.any(row_index[:, None] == polar_rows[None, :], axis=1)
    return jnp.where(listed[:, None], damping, 1.0)


def north_of(field):
    return jnp.concatenate([field[..., 1:, :], jnp.zeros_like(field[..., :1, :])], axis=-2)


def south_of(field):
    return jnp.concatenate([jnp.zeros_like(field[..., :1, :]), field[..., :-1, :]], axis=-2)


def atmos_step(tracer_now, wind_u, wind_v):
    east_side = jnp.roll(tracer_now, -1, axis=-1)
    west_side = jnp.roll(tracer_now, 1, axis=-1)
    north_side = north_of(tracer_now)
    south_side = south_of(tracer_now)
    advect = wind_u * (east_side - west_side) + wind_v * (north_side - south_side)
    spread_sum = east_side + west_side + north_side + south_side - 4.0 * tracer_now
    return tracer_now - advect_coef * advect + diffuse_coef * spread_sum


def ocean_step(temp, sea, air_temp, air_speed):
    top_level = temp[0] + sea * flux_coef * air_speed * (air_temp - temp[0])
    temp = jnp.concatenate([top_level[None], temp[1:]], axis=0)
    lateral = sea * (jnp.roll(sea, -1, axis=-1) * (jnp.roll(temp, -1, axis=-1) - temp)
                     + jnp.roll(sea, 1, axis=-1) * (jnp.roll(temp, 1, axis=-1) - temp)
                     + north_of(sea) * (north_of(temp) - temp)
                     + south_of(sea) * (south_of(temp) - temp))
    temp = temp + ocean_diffuse * lateral
    upper = jnp.concatenate([temp[:1], temp[:-1]], axis=0)
    lower = jnp.concatenate([temp[1:], temp[-1:]], axis=0)
    return temp + vertical_mix * sea * (upper + lower - 2.0 * temp)


def reference(tracer, wind_u, wind_v, ocean_temp, land_mask, remap_rows, remap_cols, polar_rows):
    wave_numbers = jnp.arange(NLON // 2 + 1).astype(jnp.float32)
    table = damp_table(jnp.arange(NLAT).astype(jnp.int32), polar_rows, wave_numbers)
    tracer_now = tracer
    for step_index in range(STEPS):
        tracer_now = atmos_step(tracer_now, wind_u, wind_v)
        spectrum = jnp.fft.rfft(tracer_now, axis=2)
        tracer_now = jnp.fft.irfft(spectrum * table[None], n=NLON, axis=2).astype(tracer.dtype)
    bottom_temp = tracer_now[LEV - 1]
    bottom_speed = jnp.abs(wind_u[LEV - 1]) + jnp.abs(wind_v[LEV - 1]) + 0.5
    air_temp = bottom_temp[remap_rows, remap_cols]
    air_speed = bottom_speed[remap_rows, remap_cols]
    sea = land_mask.astype(jnp.float32)
    temp = ocean_temp
    for step_index in range(OSTEPS):
        temp = ocean_step(temp, sea, air_temp, air_speed)
    return tracer_now, temp
```

```python
import math

import jax
import jax.numpy as jnp
import numpy as np
from jax import lax
from jax.experimental import pallas as pl
from jax.experimental.pallas import tpu as pltpu
from jax.sharding import PartitionSpec as P


f32 = jnp.float32
bf16 = jnp.bfloat16
LEV, ROWS, COLS, LONS = 32, 24, 288, 4
NLON = COLS * LONS
LB = LEV // LONS
HALF = NLON // 2
OLEV, OROWS, OCOLS = 4, 32, 896
WROWS, WCOLS = 40, 1024
WIN = 32
FT = 54 * 8

advect_coef = 0.2
diffuse_coef = 0.1
flux_coef = 0.25
ocean_diffuse = 0.15
vertical_mix = 0.2


def call(kernel, out_shape, smem=0, n_in=0, n_any=0, scratch=(), cost=None, mib=24):
    specs = [pl.BlockSpec(memory_space=pltpu.SMEM)] * smem + [pl.BlockSpec(memory_space=pltpu.VMEM)] * n_in
    specs += [pl.BlockSpec(memory_space=pl.ANY)] * n_any
    return pl.pallas_call(
        kernel,
        out_shape=out_shape,
        in_specs=specs,
        scratch_shapes=scratch,
        cost_estimate=cost,
        compiler_params=pltpu.CompilerParams(vmem_limit_bytes=mib << 20),
    )


def cost(us):
    return pl.CostEstimate(flops=0, transcendentals=0, bytes_accessed=int(us * 3.0e6))


def sds(*shape, dtype=f32):
    return jax.ShapeDtypeStruct(shape, dtype)


LEVEL_AT, OCEAN_AT, SEA_AT, LAT_WIRE = 288, 312, 368, 384
WIND_AT, STRIP_AT, RIM_WIRE = 144, 360, 400
TILES = OCOLS // 128


def pack_kernel(place, q_in, u_in, v_in, t_in, mask_in, a0, a1, a2, a3, b0, b1, b2, b3, up, down, mid, q, u, v, t, mask, sems):
    copies = [
        [
            pltpu.make_async_copy(source.at[pl.ds(LB * i, LB)], target.at[pl.ds(LB * i, LB)], sems.at[f, i])
            for i in range(LONS)
        ]
        for f, (source, target) in enumerate(((q_in, q), (u_in, u), (v_in, v)))
    ]
    copies.append([pltpu.make_async_copy(t_in, t, sems.at[3, 0]), pltpu.make_async_copy(mask_in, mask, sems.at[3, 1])])
    for group in copies:
        for copy in group:
            copy.start()
    first_wires, second_wires = (a0, a1, a2, a3), (b0, b1, b2, b3)
    for f, field in enumerate((q, u, v)):
        for copy in copies[f]:
            copy.wait()
        for s in range(LONS):
            wire, base = (first_wires[s], 0) if f == 0 else (second_wires[s], (f - 1) * FT)
            first = (place[0] + s) % LONS * LB
            for l in range(LB):
                for c in range(2):
                    wire[pl.ds(base + c * 192 + l, ROWS, stride=8), :] = field[first + l, :, c * 128 : c * 128 + 128]
                wire[pl.ds(base + 384 + l, 6, stride=8), :] = jnp.concatenate(
                    [field[first + l, 6 * i : 6 * i + 6, 256:288] for i in range(4)], axis=1
                )
    for copy in copies[3]:
        copy.wait()
    for s in range(LONS):
        first = (place[0] + s) % LONS * LB
        for l in range(LB):
            for out, rows in ((up, (22, 23, 23, 23)), (down, (0, 1, 0, 0))):
                rems = []
                for i, (field, r) in enumerate(zip((q, q, u, v), rows)):
                    for c in range(2):
                        out[pl.ds(s * 72 + c * 32 + i * 8 + l, 1), :] = field[
                            first + l, r : r + 1, c * 128 : c * 128 + 128
                        ]
                    rems.append(field[first + l, r : r + 1, 256:288])
                out[pl.ds(s * 72 + 64 + l, 1), :] = jnp.concatenate(rems, axis=1)
    for out, a, b, o in ((up, ROWS - 3, ROWS - 2, OROWS - 2), (down, 0, 0, 0)):
        for at, field, r, n in ((0, q, a, 3), (3, u, b, 2), (5, v, b, 2)):
            for c in range(2):
                out[LEVEL_AT + 8 * c + at : LEVEL_AT + 8 * c + at + n, :] = field[
                    LEV - 1, r : r + n, c * 128 : c * 128 + 128
                ]
            out[LEVEL_AT + 16 + at : LEVEL_AT + 16 + at + n, 0:32] = field[LEV - 1, r : r + n, 256:288]
        for c in range(TILES):
            for l in range(OLEV):
                out[OCEAN_AT + 8 * c + 2 * l : OCEAN_AT + 8 * c + 2 * l + 2, :] = t[
                    l, o : o + 2, c * 128 : c * 128 + 128
                ]
            out[SEA_AT + 2 * c : SEA_AT + 2 * c + 2, :] = mask[o : o + 2, c * 128 : c * 128 + 128].astype(f32)
    for f, field in enumerate((q, u, v)):
        mid[f, :, :] = field[LEV - 1, :, :]


def join_kernel(before, after, mid, t, mask, w0, w1, w2, w3, win):
    wires = (w0, w1, w2, w3)
    for s, wire in enumerate(wires):
        wire[0:72, :] = before[s * 72 : s * 72 + 72, :]
        wire[72:144, :] = after[s * 72 : s * 72 + 72, :]
    for f, (at, n) in enumerate(((0, 3), (3, 2), (5, 2))):
        win[...] = jnp.zeros((WIN, 384), f32)
        win[4 : 4 + ROWS, 0:COLS] = mid[f, :, :]
        for c in range(3):
            rows = LEVEL_AT + 8 * c + at
            width = 128 if c < 2 else 32
            win[4 - n : 4, c * 128 : c * 128 + width] = before[rows : rows + n, 0:width]
            win[4 + ROWS : 4 + ROWS + n, c * 128 : c * 128 + width] = after[rows : rows + n, 0:width]
        rem = jnp.concatenate([win[8 * i : 8 * i + 8, 256:288] for i in range(4)], axis=1)
        for wire in wires:
            base = WIND_AT + f * 72
            wire[base : base + 32, :] = win[:, 0:128]
            wire[base + 32 : base + 64, :] = win[:, 128:256]
            wire[base + 64 : base + 72, :] = rem
    pad = 128 - 2 * (OLEV + 1)
    for wire, col in ((w3, 0), (w1, OCOLS - 2)):
        tile, lane = col // 128, col % 128
        own = [t[l, :, col : col + 2] for l in range(OLEV)] + [mask[:, col : col + 2].astype(f32)]
        wire[STRIP_AT : STRIP_AT + OROWS, :] = jnp.concatenate(own + [jnp.zeros((OROWS, pad), f32)], axis=1)
        wire[STRIP_AT + OROWS : STRIP_AT + WROWS, :] = jnp.zeros((WROWS - OROWS, 128), f32)
        for near, row in ((after, OROWS), (before, WROWS - 2)):
            base = OCEAN_AT + 8 * tile
            far = [near[base + 2 * l : base + 2 * l + 2, lane : lane + 2] for l in range(OLEV)]
            far.append(near[SEA_AT + 2 * tile : SEA_AT + 2 * tile + 2, lane : lane + 2])
            wire[STRIP_AT + row : STRIP_AT + row + 2, :] = jnp.concatenate(far + [jnp.zeros((2, pad), f32)], axis=1)


def unpack_kernel(place, w0, w1, w2, w3, out):
    for s, wire in enumerate((w0, w1, w2, w3)):
        first = (place[0] + LONS - s) % LONS * LB
        for l in range(LB):
            for c in range(2):
                out[first + l, :, c * 128 : c * 128 + 128] = wire[pl.ds(c * 192 + l, ROWS, stride=8), :]
            rem = wire[pl.ds(384 + l, 6, stride=8), :]
            for i in range(4):
                out[first + l, 6 * i : 6 * i + 6, 256:288] = rem[:, 32 * i : 32 * i + 32]


def wave_tables():
    slots = np.arange(NLON)[None, :]
    wave = np.where(slots <= HALF, slots, slots - HALF)
    coarse = (32 * np.arange(36)[:, None] * wave) % NLON * (2 * np.pi / NLON)
    fine = (np.arange(32)[:, None] * wave) % NLON * (2 * np.pi / NLON)
    with_cos = np.where(slots <= HALF, np.cos(coarse), np.sin(coarse))
    with_sin = np.where(slots <= HALF, -np.sin(coarse), np.cos(coarse))
    return tuple(a.astype(np.float32) for a in (with_cos, with_sin, np.cos(fine), np.sin(fine)))


def basis_kernel(with_cos, with_sin, cosine, sine, hi, lo):
    def body(a, carry):
        row = pl.multiple_of(a * 32, 32)
        for h in (0, 16):
            value = with_cos[pl.ds(a, 1), :] * cosine[h : h + 16, :] + with_sin[pl.ds(a, 1), :] * sine[h : h + 16, :]
            top = value.astype(bf16)
            hi[pl.ds(row + h, 16), :] = top
            lo[pl.ds(row + h, 16), :] = (value - top.astype(f32)).astype(bf16)
        return carry

    lax.fori_loop(0, 36, body, 0)


def split(x):
    top = x.astype(bf16)
    return top, (x - top.astype(f32)).astype(bf16)


def product(x, hi, lo, back=False):
    top, rest = split(x)
    lines = x.shape[0]
    dims = (((1,), (1 if back else 0,)), ((), ()))

    def dot(a, b):
        return lax.dot_general(a, b[...], dims, preferred_element_type=f32)

    both = dot(jnp.concatenate([top, rest], axis=0), hi)
    return both[:lines] + both[lines:] + dot(top, lo)


def advance(q, north, south, u, v):
    east = pltpu.roll(q, NLON - 1, 1)
    west = pltpu.roll(q, 1, 1)
    advect = u * (east - west) + v * (north - south)
    spread = east + west + north + south - 4.0 * q
    return q - advect_coef * advect + diffuse_coef * spread


def bottom_kernel(w0, w1, w2, w3, damp, bh, bl, heat, speed):
    def circle(f):
        base, parts = WIND_AT + f * 72, []
        for w in (w0, w1, w2, w3):
            parts += [w[base : base + 32, :], w[base + 32 : base + 64, :]]
            parts.append(
                jnp.concatenate([w[base + 64 : base + 72, 32 * i : 32 * i + 32] for i in range(4)], axis=0)
            )
        return jnp.concatenate(parts, axis=1)

    q, u, v = circle(0), circle(1), circle(2)
    wind = jnp.abs(u) + jnp.abs(v) + 0.5
    for _ in range(2):
        q = advance(q, pltpu.roll(q, WIN - 1, 0), pltpu.roll(q, 1, 0), u, v)
        q = product(product(q, bh, bl) * damp[...], bh, bl, back=True)
    for out, field in ((heat, q), (speed, wind)):
        lane = lax.broadcasted_iota(jnp.int32, (WIN, 128), 1)
        out[:, 0:256] = field[:, 0:256]
        out[:, 256:384] = jnp.where(lane < 64, field[:, 256:384], field[:, NLON - 128 : NLON])


def bulk_kernel(m0, m1, m2, m3, n0, n1, n2, n3, h0, h1, h2, h3, damp, bh, bl, after, o0, o1, o2, o3, qs, us, vs, xs):
    halos = (h0, h1, h2, h3)

    def main_slab(f, r):
        parts = []
        for w in (m0, m1, m2, m3) if f == 0 else (n0, n1, n2, n3):
            base = max(f - 1, 0) * FT
            parts.append(w[base + r * 8 : base + r * 8 + 8, :])
            parts.append(w[base + 192 + r * 8 : base + 200 + r * 8, :])
            g, i = r % 6, r // 6
            parts.append(w[base + 384 + g * 8 : base + 392 + g * 8, 32 * i : 32 * i + 32])
        return jnp.concatenate(parts, axis=1)

    def halo_slab(side, i):
        parts = []
        for h in halos:
            base = side * 72
            parts.append(h[base + i * 8 : base + i * 8 + 8, :])
            parts.append(h[base + 32 + i * 8 : base + 40 + i * 8, :])
            parts.append(h[base + 64 : base + 72, 32 * i : 32 * i + 32])
        return jnp.concatenate(parts, axis=1)

    def put(ref, slot, value):
        ref[slot * 8 : slot * 8 + 8, :] = value

    for r in range(ROWS):
        put(qs, r + 2, main_slab(0, r))
        put(us, r + 1, main_slab(1, r))
        put(vs, r + 1, main_slab(2, r))
    put(qs, 0, halo_slab(0, 0))
    put(qs, 1, halo_slab(0, 1))
    put(us, 0, halo_slab(0, 2))
    put(vs, 0, halo_slab(0, 3))
    put(qs, 26, halo_slab(1, 0))
    put(qs, 27, halo_slab(1, 1))
    put(us, 25, halo_slab(1, 2))
    put(vs, 25, halo_slab(1, 3))

    def at(ref, slot):
        return ref[pl.ds(pl.multiple_of(slot * 8, 8), 8), :]

    def scale(count, first):
        def body(r, carry):
            xs[pl.ds(pl.multiple_of(r * 8, 8), 8), :] = at(xs, r) * damp[pl.ds(r + first, 1), :]
            return carry

        lax.fori_loop(0, count, body, 0)

    def first(r, carry):
        xs[pl.ds(pl.multiple_of(r * 8, 8), 8), :] = advance(
            at(qs, r + 1), at(qs, r + 2), at(qs, r), at(us, r), at(vs, r)
        )
        return carry

    lax.fori_loop(0, ROWS + 2, first, 0)
    xs[...] = product(xs[...], bh, bl)
    scale(ROWS + 2, 3)
    qs[0:208, :] = product(xs[...], bh, bl, back=True)

    def second(r, carry):
        xs[pl.ds(pl.multiple_of(r * 8, 8), 8), :] = advance(
            at(qs, r + 1), at(qs, r + 2), at(qs, r), at(us, r + 1), at(vs, r + 1)
        )
        return carry

    lax.fori_loop(0, ROWS, second, 0)
    xs[0:192, :] = product(xs[0:192, :], bh, bl)
    scale(ROWS, 4)
    xs[0:192, :] = product(xs[0:192, :], bh, bl, back=True)
    for p, out in enumerate((o0, o1, o2, o3)):
        for g in range(6):
            rems = []
            for r in range(g, ROWS, 6):
                piece = xs[r * 8 : r * 8 + 8, p * COLS : p * COLS + COLS]
                out[r * 8 : r * 8 + 8, :] = piece[:, 0:128]
                out[192 + r * 8 : 200 + r * 8, :] = piece[:, 128:256]
                rems.append(piece[:, 256:288])
            out[384 + g * 8 : 392 + g * 8, :] = jnp.concatenate(rems, axis=1)


def pick_kernel(place, rows, cols, heat, speed, air_heat, air_speed, up, down):
    def body(k, carry):
        start = pl.multiple_of(k * 8, 8)
        for c in range(TILES):
            row = rows[pl.ds(start, 8), c * 128 : c * 128 + 128] - place[1] * ROWS + 4
            col = cols[pl.ds(start, 8), c * 128 : c * 128 + 128] - place[0] * COLS
            col = jnp.where(col < 0, col + NLON, col)
            col = jnp.where(col > COLS, col - (NLON - 384), col)
            key = row * 4 + (col >> 7)
            lane = col & 127
            got_heat = jnp.zeros((8, 128), f32)
            got_speed = jnp.zeros((8, 128), f32)
            for w in range(3, 29):
                for b in range(3):
                    mine = key == w * 4 + b
                    line_heat = jnp.broadcast_to(heat[w : w + 1, b * 128 : b * 128 + 128], (8, 128))
                    line_speed = jnp.broadcast_to(speed[w : w + 1, b * 128 : b * 128 + 128], (8, 128))
                    got_heat = jnp.where(mine, jnp.take_along_axis(line_heat, lane, axis=1), got_heat)
                    got_speed = jnp.where(mine, jnp.take_along_axis(line_speed, lane, axis=1), got_speed)
            air_heat[pl.ds(start, 8), c * 128 : c * 128 + 128] = got_heat
            air_speed[pl.ds(start, 8), c * 128 : c * 128 + 128] = got_speed
        return carry

    lax.fori_loop(0, OROWS // 8, body, 0)
    for f, field in enumerate((air_heat, air_speed)):
        up[2 * f : 2 * f + 2, :] = field[OROWS - 2 : OROWS, :]
        down[2 * f : 2 * f + 2, :] = field[0:2, :]


def ring_kernel(heat, speed, before, after, behind, east, west):
    for out, col in ((east, 0), (west, OCOLS - 2)):
        out[0:OROWS, :] = jnp.concatenate([heat[:, col : col + 2], speed[:, col : col + 2]], axis=1)
        out[OROWS:WROWS, :] = jnp.zeros((WROWS - OROWS, 4), f32)
        for near, row in ((after, OROWS), (before, WROWS - 2)):
            out[row : row + 2, :] = jnp.concatenate([near[0:2, col : col + 2], near[2:4, col : col + 2]], axis=1)


def ocean_kernel(t, mask, heat, speed, before, after, east, west, air_before, air_after, air_east, air_west, out, win):
    gap = jnp.zeros((WROWS, 124), f32)
    strip = slice(STRIP_AT, STRIP_AT + WROWS)

    def window(field, slot, above, below, right, left):
        win[slot, OROWS:WROWS, :] = jnp.zeros((WROWS - OROWS, WCOLS), f32)
        win[slot, 0:OROWS, 0:OCOLS] = field
        for c in range(TILES):
            win[slot, OROWS : OROWS + 2, c * 128 : c * 128 + 128] = below(c)
            win[slot, WROWS - 2 : WROWS, c * 128 : c * 128 + 128] = above(c)
        win[slot, :, OCOLS:WCOLS] = jnp.concatenate([right, gap, left], axis=1)
        return win[slot]

    def sea_rows(wire):
        return lambda c: wire[SEA_AT + 2 * c : SEA_AT + 2 * c + 2, :]

    def level_rows(wire, l):
        return lambda c: wire[OCEAN_AT + 8 * c + 2 * l : OCEAN_AT + 8 * c + 2 * l + 2, :]

    def air_rows(wire, f):
        return lambda c: wire[2 * f : 2 * f + 2, c * 128 : c * 128 + 128]

    temps = [
        window(
            t[l], l, level_rows(before, l), level_rows(after, l),
            east[strip, 2 * l : 2 * l + 2], west[strip, 2 * l : 2 * l + 2],
        )
        for l in range(OLEV)
    ]
    sea = window(mask[...].astype(f32), 4, sea_rows(before), sea_rows(after), east[strip, 8:10], west[strip, 8:10])
    air = [
        window(
            field[...], 5 + f, air_rows(air_before, f), air_rows(air_after, f),
            air_east[:, 2 * f : 2 * f + 2], air_west[:, 2 * f : 2 * f + 2],
        )
        for f, field in enumerate((heat, speed))
    ]

    def beside(field):
        return (
            pltpu.roll(field, WCOLS - 1, 1),
            pltpu.roll(field, 1, 1),
            pltpu.roll(field, WROWS - 1, 0),
            pltpu.roll(field, 1, 0),
        )

    seas = beside(sea)
    rate = sea * flux_coef * air[1]
    for _ in range(2):
        temps[0] = temps[0] + rate * (air[0] - temps[0])
        moved = []
        for field in temps:
            total = jnp.zeros_like(field)
            for near_sea, near in zip(seas, beside(field)):
                total = total + near_sea * (near - field)
            moved.append(field + ocean_diffuse * (sea * total))
        temps = [
            moved[l]
            + vertical_mix * sea * (moved[max(l - 1, 0)] + moved[min(l + 1, OLEV - 1)] - 2.0 * moved[l])
            for l in range(OLEV)
        ]
    for l in range(OLEV):
        out[l, :, :] = temps[l][0:OROWS, 0:OCOLS]


def damp_window(lat_place, polar_rows, lat_total, band_rows):
    slots = np.arange(NLON)
    waves = np.where(slots < HALF, slots, np.where(slots == HALF, HALF, slots - HALF))
    weight = np.where((slots == 0) | (slots == HALF), 1.0, 2.0) / NLON
    sine = np.where(waves > 0, np.sin(np.pi * waves / NLON), 1.0)
    row_index = lat_place * ROWS - 4 + jnp.arange(WIN, dtype=jnp.int32)
    latitude_cos = jnp.sin(math.pi * (row_index.astype(f32) + 0.5) / lat_total)
    ratio = latitude_cos / math.sin(math.pi * band_rows / lat_total)
    damping = jnp.minimum(1.0, ratio[:, None] / sine.astype(np.float32)[None, :])
    damping = jnp.where(waves[None, :] > 0, damping, 1.0)
    listed = jnp.any(row_index[:, None] == polar_rows[None, :], axis=1)
    inside = (row_index >= 0) & (row_index < lat_total)
    table = jnp.where(listed[:, None], damping, 1.0) * weight.astype(np.float32)[None, :]
    return jnp.where(inside[:, None], table, 0.0)


def per_device(tracer, wind_u, wind_v, ocean_temp, land_mask, remap_rows, remap_cols, polar_rows):
    lat_devices = lax.axis_size("lat")
    lat_place, lon_place = lax.axis_index("lat"), lax.axis_index("lon")
    place = jnp.stack([lon_place, lat_place]).astype(jnp.int32)
    north = [(i, i + 1) for i in range(lat_devices - 1)]
    south = [(j, i) for i, j in north]

    def along(x, s):
        return lax.ppermute(x, "lon", [(i, (i + s) % LONS) for i in range(LONS)])

    def across(to_north, to_south):
        before = lax.ppermute(to_north, "lat", north)
        return before, lax.ppermute(to_south, "lat", south)

    packed = call(
        pack_kernel,
        [sds(FT, 128)] * 4 + [sds(2 * FT, 128)] * 4 + [sds(LAT_WIRE, 128)] * 2 + [sds(3, ROWS, COLS)],
        smem=1,
        n_any=5,
        scratch=[pltpu.VMEM((LEV, ROWS, COLS), f32)] * 3
        + [
            pltpu.VMEM((OLEV, OROWS, OCOLS), f32),
            pltpu.VMEM((OROWS, OCOLS), jnp.int32),
            pltpu.SemaphoreType.DMA((4, LONS)),
        ],
        cost=cost(5),
        mib=60,
    )(place, tracer, wind_u, wind_v, ocean_temp, land_mask)
    mains, winds, mid = packed[:4], packed[4:8], packed[10]
    pieces = [mains[0]] + [along(mains[s], s) for s in (3, 2, 1)]
    before, after = across(packed[8], packed[9])

    basis = call(basis_kernel, [sds(NLON, NLON, dtype=bf16)] * 2, n_in=4, cost=cost(3))(*wave_tables())
    damp = damp_window(lat_place, polar_rows, ROWS * lat_devices, lat_devices // 8 * ROWS)
    joined = call(
        join_kernel,
        [sds(RIM_WIRE if s in (1, 3) else STRIP_AT, 128) for s in range(LONS)],
        n_in=5,
        scratch=[pltpu.VMEM((WIN, 384), f32)],
        cost=cost(2),
    )(before, after, mid, ocean_temp, land_mask)
    rims = [joined[0]] + [along(joined[s], s) for s in (3, 2, 1)]
    blows = [winds[0]] + [along(winds[s], s) for s in (3, 2, 1)]

    heat, speed = call(bottom_kernel, [sds(WIN, 384)] * 2, n_in=7, cost=cost(8))(*rims, damp, *basis)
    air_heat, air_speed, air_up, air_down = call(
        pick_kernel, [sds(OROWS, OCOLS)] * 2 + [sds(4, OCOLS)] * 2, smem=1, n_in=4, cost=cost(7)
    )(place, remap_rows, remap_cols, heat, speed)
    air_before, air_after = across(air_up, air_down)

    lines = (ROWS + 4) * LB
    outs = call(
        bulk_kernel,
        [sds(FT, 128)] * 4,
        n_in=15,
        n_any=1,
        scratch=[pltpu.VMEM((lines, NLON), f32)] + [pltpu.VMEM((lines - 16, NLON), f32)] * 3,
        cost=cost(18),
        mib=36,
    )(*pieces, *blows, *rims, damp, *basis, air_up)
    back = [outs[0]] + [along(outs[s], s) for s in (1, 2, 3)]

    east, west = call(ring_kernel, [sds(WROWS, 4)] * 2, n_in=4, n_any=1, cost=cost(1))(
        air_heat, air_speed, air_before, air_after, outs[0]
    )
    air_east, air_west = along(east, LONS - 1), along(west, 1)
    ocean_out = call(
        ocean_kernel, sds(OLEV, OROWS, OCOLS), n_in=12, scratch=[pltpu.VMEM((7, WROWS, WCOLS), f32)], cost=cost(3)
    )(
        ocean_temp, land_mask, air_heat, air_speed, before, after, rims[1], rims[3],
        air_before, air_after, air_east, air_west,
    )
    tracer_out = call(unpack_kernel, sds(LEV, ROWS, COLS), smem=1, n_in=4, cost=cost(2))(place, *back)
    return tracer_out, ocean_out


def solution(mesh):
    band = P(None, "lat", "lon")
    cells = P("lat", "lon")
    return jax.shard_map(
        per_device,
        mesh=mesh,
        in_specs=(band, band, band, band, cells, cells, cells, P()),
        out_specs=(band, band),
        check_vma=False,
    )
```

```python
import math

import jax
import jax.numpy as jnp
import numpy as np
from jax import lax
from jax.experimental import pallas as pl
from jax.experimental.pallas import tpu as pltpu
from jax.sharding import PartitionSpec as P


f32 = jnp.float32
bf16 = jnp.bfloat16
LEV, ROWS, COLS, LONS = 32, 24, 288, 4
NLON = COLS * LONS
LB = LEV // LONS
HALF = NLON // 2
OLEV, OROWS, OCOLS = 4, 32, 896
WROWS, WCOLS = 40, 1024
WIN = 32
FT = 54 * 8

advect_coef = 0.2
diffuse_coef = 0.1
flux_coef = 0.25
ocean_diffuse = 0.15
vertical_mix = 0.2


def call(kernel, out_shape, smem=0, n_in=0, n_any=0, scratch=(), cost=None, mib=24):
    specs = [pl.BlockSpec(memory_space=pltpu.SMEM)] * smem + [pl.BlockSpec(memory_space=pltpu.VMEM)] * n_in
    specs += [pl.BlockSpec(memory_space=pl.ANY)] * n_any
    return pl.pallas_call(
        kernel,
        out_shape=out_shape,
        in_specs=specs,
        scratch_shapes=scratch,
        cost_estimate=cost,
        compiler_params=pltpu.CompilerParams(vmem_limit_bytes=mib << 20),
    )


def cost(us):
    return pl.CostEstimate(flops=0, transcendentals=0, bytes_accessed=int(us * 3.0e6))


def sds(*shape, dtype=f32):
    return jax.ShapeDtypeStruct(shape, dtype)


LEVEL_AT, OCEAN_AT, SEA_AT, LAT_WIRE = 288, 312, 368, 384
FIRST, SECOND = FT + 192, 2 * FT - 192
STRIP_AT, RIM_WIRE, WINDOW = 144, 184, 216
TILES = OCOLS // 128


def wire_places(f, first, second):
    if f == 0:
        return ((first, 0), (first, 192), (first, 384))
    if f == 1:
        return ((first, FT), (second, 0), (second, 192))
    return ((second, 240), (second, 432), (second, 624))


def cross(place, a, b, first, second):
    odd = jnp.full(a.shape, place[1] % 2, jnp.int32) == 1
    first[...] = jnp.where(odd, a[...], b[...])
    second[...] = jnp.where(odd, b[...], a[...])


def pack_kernel(place, q_in, u_in, v_in, t_in, mask_in, a0, a1, a2, a3, b0, b1, b2, b3, x0, x1, mid, q, u, v, t, mask, up, down, sems):
    copies = [
        [
            pltpu.make_async_copy(source.at[pl.ds(LB * i, LB)], target.at[pl.ds(LB * i, LB)], sems.at[f, i])
            for i in range(LONS)
        ]
        for f, (source, target) in enumerate(((q_in, q), (u_in, u), (v_in, v)))
    ]
    copies.append([pltpu.make_async_copy(t_in, t, sems.at[3, 0]), pltpu.make_async_copy(mask_in, mask, sems.at[3, 1])])
    for group in copies:
        for copy in group:
            copy.start()
    first_wires, second_wires = (a0, a1, a2, a3), (b0, b1, b2, b3)
    for f, field in enumerate((q, u, v)):
        for copy in copies[f]:
            copy.wait()
        for s in range(LONS):
            places = wire_places(f, first_wires[s], second_wires[s])
            first = (place[0] + s) % LONS * LB
            for l in range(LB):
                for c in range(2):
                    wire, base = places[c]
                    wire[pl.ds(base + l, ROWS, stride=8), :] = field[first + l, :, c * 128 : c * 128 + 128]
                wire, base = places[2]
                wire[pl.ds(base + l, 6, stride=8), :] = jnp.concatenate(
                    [field[first + l, 6 * i : 6 * i + 6, 256:288] for i in range(4)], axis=1
                )
    for copy in copies[3]:
        copy.wait()
    for s in range(LONS):
        first = (place[0] + s) % LONS * LB
        for l in range(LB):
            for out, rows in ((up, (22, 23, 23, 23)), (down, (0, 1, 0, 0))):
                rems = []
                for i, (field, r) in enumerate(zip((q, q, u, v), rows)):
                    for c in range(2):
                        out[pl.ds(s * 72 + c * 32 + i * 8 + l, 1), :] = field[
                            first + l, r : r + 1, c * 128 : c * 128 + 128
                        ]
                    rems.append(field[first + l, r : r + 1, 256:288])
                out[pl.ds(s * 72 + 64 + l, 1), :] = jnp.concatenate(rems, axis=1)
    for out, a, b, o in ((up, ROWS - 3, ROWS - 2, OROWS - 2), (down, 0, 0, 0)):
        for at, field, r, n in ((0, q, a, 3), (3, u, b, 2), (5, v, b, 2)):
            for c in range(2):
                out[LEVEL_AT + 8 * c + at : LEVEL_AT + 8 * c + at + n, :] = field[
                    LEV - 1, r : r + n, c * 128 : c * 128 + 128
                ]
            out[LEVEL_AT + 16 + at : LEVEL_AT + 16 + at + n, 0:32] = field[LEV - 1, r : r + n, 256:288]
        for c in range(TILES):
            for l in range(OLEV):
                out[OCEAN_AT + 8 * c + 2 * l : OCEAN_AT + 8 * c + 2 * l + 2, :] = t[
                    l, o : o + 2, c * 128 : c * 128 + 128
                ]
            out[SEA_AT + 2 * c : SEA_AT + 2 * c + 2, :] = mask[o : o + 2, c * 128 : c * 128 + 128].astype(f32)
    for f, field in enumerate((q, u, v)):
        mid[f, :, :] = field[LEV - 1, :, :]
    cross(place, up, down, x0, x1)


def join_kernel(place, x0, x1, mid, t, mask, w0, w1, w2, w3, circle, before, after, win):
    cross(place, x1, x0, before, after)
    wires = (w0, w1, w2, w3)
    for s, wire in enumerate(wires):
        wire[0:72, :] = before[s * 72 : s * 72 + 72, :]
        wire[72:144, :] = after[s * 72 : s * 72 + 72, :]
    for f, (at, n) in enumerate(((0, 3), (3, 2), (5, 2))):
        win[...] = jnp.zeros((WIN, 384), f32)
        win[4 : 4 + ROWS, 0:COLS] = mid[f, :, :]
        for c in range(3):
            rows = LEVEL_AT + 8 * c + at
            width = 128 if c < 2 else 32
            win[4 - n : 4, c * 128 : c * 128 + width] = before[rows : rows + n, 0:width]
            win[4 + ROWS : 4 + ROWS + n, c * 128 : c * 128 + width] = after[rows : rows + n, 0:width]
        rem = jnp.concatenate([win[8 * i : 8 * i + 8, 256:288] for i in range(4)], axis=1)
        circle[f * 72 : f * 72 + 32, :] = win[:, 0:128]
        circle[f * 72 + 32 : f * 72 + 64, :] = win[:, 128:256]
        circle[f * 72 + 64 : f * 72 + 72, :] = rem
    pad = 128 - 2 * (OLEV + 1)
    for wire, col in ((w3, 0), (w1, OCOLS - 2)):
        tile, lane = col // 128, col % 128
        own = [t[l, :, col : col + 2] for l in range(OLEV)] + [mask[:, col : col + 2].astype(f32)]
        wire[STRIP_AT : STRIP_AT + OROWS, :] = jnp.concatenate(own + [jnp.zeros((OROWS, pad), f32)], axis=1)
        wire[STRIP_AT + OROWS : STRIP_AT + WROWS, :] = jnp.zeros((WROWS - OROWS, 128), f32)
        for near, row in ((after, OROWS), (before, WROWS - 2)):
            base = OCEAN_AT + 8 * tile
            far = [near[base + 2 * l : base + 2 * l + 2, lane : lane + 2] for l in range(OLEV)]
            far.append(near[SEA_AT + 2 * tile : SEA_AT + 2 * tile + 2, lane : lane + 2])
            wire[STRIP_AT + row : STRIP_AT + row + 2, :] = jnp.concatenate(far + [jnp.zeros((2, pad), f32)], axis=1)


def unpack_kernel(place, w0, w1, w2, w3, out):
    for s, wire in enumerate((w0, w1, w2, w3)):
        first = (place[0] + LONS - s) % LONS * LB
        for l in range(LB):
            for c in range(2):
                out[first + l, :, c * 128 : c * 128 + 128] = wire[pl.ds(c * 192 + l, ROWS, stride=8), :]
            rem = wire[pl.ds(384 + l, 6, stride=8), :]
            for i in range(4):
                out[first + l, 6 * i : 6 * i + 6, 256:288] = rem[:, 32 * i : 32 * i + 32]


def wave_tables():
    slots = np.arange(NLON)[None, :]
    wave = np.where(slots <= HALF, slots, slots - HALF)
    coarse = (32 * np.arange(36)[:, None] * wave) % NLON * (2 * np.pi / NLON)
    fine = (np.arange(32)[:, None] * wave) % NLON * (2 * np.pi / NLON)
    with_cos = np.where(slots <= HALF, np.cos(coarse), np.sin(coarse))
    with_sin = np.where(slots <= HALF, -np.sin(coarse), np.cos(coarse))
    return tuple(a.astype(np.float32) for a in (with_cos, with_sin, np.cos(fine), np.sin(fine)))


def basis_kernel(with_cos, with_sin, cosine, sine, hi, lo):
    def body(a, carry):
        row = pl.multiple_of(a * 32, 32)
        for h in (0, 16):
            value = with_cos[pl.ds(a, 1), :] * cosine[h : h + 16, :] + with_sin[pl.ds(a, 1), :] * sine[h : h + 16, :]
            top = value.astype(bf16)
            hi[pl.ds(row + h, 16), :] = top
            lo[pl.ds(row + h, 16), :] = (value - top.astype(f32)).astype(bf16)
        return carry

    lax.fori_loop(0, 36, body, 0)


def split(x):
    top = x.astype(bf16)
    return top, (x - top.astype(f32)).astype(bf16)


def product(x, hi, lo, back=False):
    top, rest = split(x)
    lines = x.shape[0]
    dims = (((1,), (1 if back else 0,)), ((), ()))

    def dot(a, b):
        return lax.dot_general(a, b[...], dims, preferred_element_type=f32)

    both = dot(jnp.concatenate([top, rest], axis=0), hi)
    return both[:lines] + both[lines:] + dot(top, lo)


def advance(q, north, south, u, v):
    east = pltpu.roll(q, NLON - 1, 1)
    west = pltpu.roll(q, 1, 1)
    advect = u * (east - west) + v * (north - south)
    spread = east + west + north + south - 4.0 * q
    return q - advect_coef * advect + diffuse_coef * spread


def bottom_kernel(w0, w1, w2, w3, damp, bh, bl, heat, speed):
    def circle(f):
        base, parts = f * 72, []
        for w in (w0, w1, w2, w3):
            parts += [w[base : base + 32, :], w[base + 32 : base + 64, :]]
            parts.append(
                jnp.concatenate([w[base + 64 : base + 72, 32 * i : 32 * i + 32] for i in range(4)], axis=0)
            )
        return jnp.concatenate(parts, axis=1)

    q, u, v = circle(0), circle(1), circle(2)
    wind = jnp.abs(u) + jnp.abs(v) + 0.5
    for _ in range(2):
        q = advance(q, pltpu.roll(q, WIN - 1, 0), pltpu.roll(q, 1, 0), u, v)
        q = product(product(q, bh, bl) * damp[...], bh, bl, back=True)
    for out, field in ((heat, q), (speed, wind)):
        lane = lax.broadcasted_iota(jnp.int32, (WIN, 128), 1)
        out[:, 0:256] = field[:, 0:256]
        out[:, 256:384] = jnp.where(lane < 64, field[:, 256:384], field[:, NLON - 128 : NLON])


def bulk_kernel(m0, m1, m2, m3, n0, n1, n2, n3, h0, h1, h2, h3, damp, bh, bl, after, far, top_out, rest_out, qs, us, vs, xs):
    halos = (h0, h1, h2, h3)

    def main_slab(f, r):
        parts = []
        for first, second in zip((m0, m1, m2, m3), (n0, n1, n2, n3)):
            (w0, at0), (w1, at1), (w2, at2) = wire_places(f, first, second)
            g, i = r % 6, r // 6
            parts.append(w0[at0 + r * 8 : at0 + r * 8 + 8, :])
            parts.append(w1[at1 + r * 8 : at1 + r * 8 + 8, :])
            parts.append(w2[at2 + g * 8 : at2 + g * 8 + 8, 32 * i : 32 * i + 32])
        return jnp.concatenate(parts, axis=1)

    def halo_slab(side, i):
        parts = []
        for h in halos:
            base = side * 72
            parts.append(h[base + i * 8 : base + i * 8 + 8, :])
            parts.append(h[base + 32 + i * 8 : base + 40 + i * 8, :])
            parts.append(h[base + 64 : base + 72, 32 * i : 32 * i + 32])
        return jnp.concatenate(parts, axis=1)

    def put(ref, slot, value):
        ref[slot * 8 : slot * 8 + 8, :] = value

    for r in range(ROWS):
        put(qs, r + 2, main_slab(0, r))
        put(us, r + 1, main_slab(1, r))
        put(vs, r + 1, main_slab(2, r))
    put(qs, 0, halo_slab(0, 0))
    put(qs, 1, halo_slab(0, 1))
    put(us, 0, halo_slab(0, 2))
    put(vs, 0, halo_slab(0, 3))
    put(qs, 26, halo_slab(1, 0))
    put(qs, 27, halo_slab(1, 1))
    put(us, 25, halo_slab(1, 2))
    put(vs, 25, halo_slab(1, 3))

    def at(ref, slot):
        return ref[pl.ds(pl.multiple_of(slot * 8, 8), 8), :]

    def scale(count, first):
        def body(r, carry):
            xs[pl.ds(pl.multiple_of(r * 8, 8), 8), :] = at(xs, r) * damp[pl.ds(r + first, 1), :]
            return carry

        lax.fori_loop(0, count, body, 0)

    def first(r, carry):
        xs[pl.ds(pl.multiple_of(r * 8, 8), 8), :] = advance(
            at(qs, r + 1), at(qs, r + 2), at(qs, r), at(us, r), at(vs, r)
        )
        return carry

    lax.fori_loop(0, ROWS + 2, first, 0)
    xs[...] = product(xs[...], bh, bl)
    scale(ROWS + 2, 3)
    qs[0:208, :] = product(xs[...], bh, bl, back=True)

    def second(r, carry):
        xs[pl.ds(pl.multiple_of(r * 8, 8), 8), :] = advance(
            at(qs, r + 1), at(qs, r + 2), at(qs, r), at(us, r + 1), at(vs, r + 1)
        )
        return carry

    lax.fori_loop(0, ROWS, second, 0)
    xs[0:192, :] = product(xs[0:192, :], bh, bl)
    scale(ROWS, 4)
    top, rest = split(xs[0:192, :])
    top_out[...] = top
    rest_out[...] = rest
    write_piece(far, project(top, rest, bh[2 * COLS : 3 * COLS, :], bl[2 * COLS : 3 * COLS, :]))


def project(top, rest, hi, lo):
    dims = (((1,), (1,)), ((), ()))
    lines = top.shape[0]
    both = lax.dot_general(jnp.concatenate([top, rest], axis=0), hi, dims, preferred_element_type=f32)
    return both[:lines] + both[lines:] + lax.dot_general(top, lo, dims, preferred_element_type=f32)


def write_piece(out, piece):
    for g in range(6):
        rems = []
        for r in range(g, ROWS, 6):
            out[r * 8 : r * 8 + 8, :] = piece[r * 8 : r * 8 + 8, 0:128]
            out[192 + r * 8 : 200 + r * 8, :] = piece[r * 8 : r * 8 + 8, 128:256]
            rems.append(piece[r * 8 : r * 8 + 8, 256:288])
        out[384 + g * 8 : 392 + g * 8, :] = jnp.concatenate(rems, axis=1)


def finish_kernel(top, rest, bh, bl, o0, o1, o3):
    for out, p in ((o3, 3), (o1, 1), (o0, 0)):
        rows = slice(p * COLS, p * COLS + COLS)
        write_piece(out, project(top[...], rest[...], bh[rows, :], bl[rows, :]))


def pick_kernel(place, rows, cols, heat, speed, air_heat, air_speed, x0, x1, up, down):
    def body(k, carry):
        start = pl.multiple_of(k * 8, 8)
        for c in range(TILES):
            row = rows[pl.ds(start, 8), c * 128 : c * 128 + 128] - place[1] * ROWS + 4
            col = cols[pl.ds(start, 8), c * 128 : c * 128 + 128] - place[0] * COLS
            col = jnp.where(col < 0, col + NLON, col)
            col = jnp.where(col > COLS, col - (NLON - 384), col)
            key = row * 4 + (col >> 7)
            lane = col & 127
            got_heat = jnp.zeros((8, 128), f32)
            got_speed = jnp.zeros((8, 128), f32)
            for w in range(3, 29):
                for b in range(3):
                    mine = key == w * 4 + b
                    line_heat = jnp.broadcast_to(heat[w : w + 1, b * 128 : b * 128 + 128], (8, 128))
                    line_speed = jnp.broadcast_to(speed[w : w + 1, b * 128 : b * 128 + 128], (8, 128))
                    got_heat = jnp.where(mine, jnp.take_along_axis(line_heat, lane, axis=1), got_heat)
                    got_speed = jnp.where(mine, jnp.take_along_axis(line_speed, lane, axis=1), got_speed)
            air_heat[pl.ds(start, 8), c * 128 : c * 128 + 128] = got_heat
            air_speed[pl.ds(start, 8), c * 128 : c * 128 + 128] = got_speed
        return carry

    lax.fori_loop(0, OROWS // 8, body, 0)
    for f, field in enumerate((air_heat, air_speed)):
        up[2 * f : 2 * f + 2, :] = field[OROWS - 2 : OROWS, :]
        down[2 * f : 2 * f + 2, :] = field[0:2, :]
    cross(place, up, down, x0, x1)


def ring_kernel(place, heat, speed, x0, x1, behind, east, west, before, after):
    cross(place, x1, x0, before, after)
    for out, col in ((east, 0), (west, OCOLS - 2)):
        out[0:OROWS, :] = jnp.concatenate([heat[:, col : col + 2], speed[:, col : col + 2]], axis=1)
        out[OROWS:WROWS, :] = jnp.zeros((WROWS - OROWS, 4), f32)
        for near, row in ((after, OROWS), (before, WROWS - 2)):
            out[row : row + 2, :] = jnp.concatenate([near[0:2, col : col + 2], near[2:4, col : col + 2]], axis=1)


def ocean_kernel(t, mask, heat, speed, before, after, east, west, air_before, air_after, air_east, air_west, out, win):
    gap = jnp.zeros((WROWS, 124), f32)
    strip = slice(STRIP_AT, STRIP_AT + WROWS)

    def window(field, slot, above, below, right, left):
        win[slot, OROWS:WROWS, :] = jnp.zeros((WROWS - OROWS, WCOLS), f32)
        win[slot, 0:OROWS, 0:OCOLS] = field
        for c in range(TILES):
            win[slot, OROWS : OROWS + 2, c * 128 : c * 128 + 128] = below(c)
            win[slot, WROWS - 2 : WROWS, c * 128 : c * 128 + 128] = above(c)
        win[slot, :, OCOLS:WCOLS] = jnp.concatenate([right, gap, left], axis=1)
        return win[slot]

    def sea_rows(wire):
        return lambda c: wire[SEA_AT + 2 * c : SEA_AT + 2 * c + 2, :]

    def level_rows(wire, l):
        return lambda c: wire[OCEAN_AT + 8 * c + 2 * l : OCEAN_AT + 8 * c + 2 * l + 2, :]

    def air_rows(wire, f):
        return lambda c: wire[2 * f : 2 * f + 2, c * 128 : c * 128 + 128]

    temps = [
        window(
            t[l], l, level_rows(before, l), level_rows(after, l),
            east[strip, 2 * l : 2 * l + 2], west[strip, 2 * l : 2 * l + 2],
        )
        for l in range(OLEV)
    ]
    sea = window(mask[...].astype(f32), 4, sea_rows(before), sea_rows(after), east[strip, 8:10], west[strip, 8:10])
    air = [
        window(
            field[...], 5 + f, air_rows(air_before, f), air_rows(air_after, f),
            air_east[:, 2 * f : 2 * f + 2], air_west[:, 2 * f : 2 * f + 2],
        )
        for f, field in enumerate((heat, speed))
    ]

    def beside(field):
        return (
            pltpu.roll(field, WCOLS - 1, 1),
            pltpu.roll(field, 1, 1),
            pltpu.roll(field, WROWS - 1, 0),
            pltpu.roll(field, 1, 0),
        )

    seas = beside(sea)
    rate = sea * flux_coef * air[1]
    for _ in range(2):
        temps[0] = temps[0] + rate * (air[0] - temps[0])
        moved = []
        for field in temps:
            total = jnp.zeros_like(field)
            for near_sea, near in zip(seas, beside(field)):
                total = total + near_sea * (near - field)
            moved.append(field + ocean_diffuse * (sea * total))
        temps = [
            moved[l]
            + vertical_mix * sea * (moved[max(l - 1, 0)] + moved[min(l + 1, OLEV - 1)] - 2.0 * moved[l])
            for l in range(OLEV)
        ]
    for l in range(OLEV):
        out[l, :, :] = temps[l][0:OROWS, 0:OCOLS]


def damp_window(lat_place, polar_rows, lat_total, band_rows):
    slots = np.arange(NLON)
    waves = np.where(slots < HALF, slots, np.where(slots == HALF, HALF, slots - HALF))
    weight = np.where((slots == 0) | (slots == HALF), 1.0, 2.0) / NLON
    sine = np.where(waves > 0, np.sin(np.pi * waves / NLON), 1.0)
    row_index = lat_place * ROWS - 4 + jnp.arange(WIN, dtype=jnp.int32)
    latitude_cos = jnp.sin(math.pi * (row_index.astype(f32) + 0.5) / lat_total)
    ratio = latitude_cos / math.sin(math.pi * band_rows / lat_total)
    damping = jnp.minimum(1.0, ratio[:, None] / sine.astype(np.float32)[None, :])
    damping = jnp.where(waves[None, :] > 0, damping, 1.0)
    listed = jnp.any(row_index[:, None] == polar_rows[None, :], axis=1)
    inside = (row_index >= 0) & (row_index < lat_total)
    table = jnp.where(listed[:, None], damping, 1.0) * weight.astype(np.float32)[None, :]
    return jnp.where(inside[:, None], table, 0.0)


def per_device(tracer, wind_u, wind_v, ocean_temp, land_mask, remap_rows, remap_cols, polar_rows):
    lat_devices = lax.axis_size("lat")
    lat_place, lon_place = lax.axis_index("lat"), lax.axis_index("lon")
    place = jnp.stack([lon_place, lat_place]).astype(jnp.int32)
    swaps = [
        [pair for i in range(start, lat_devices - 1, 2) for pair in ((i, i + 1), (i + 1, i))] for start in (1, 0)
    ]

    def along(x, s):
        return lax.ppermute(x, "lon", [(i, (i + s) % LONS) for i in range(LONS)])

    def across(first, second):
        got = lax.ppermute(first, "lat", swaps[0])
        return got, lax.ppermute(second, "lat", swaps[1])

    packed = call(
        pack_kernel,
        [sds(FIRST, 128)] * 4 + [sds(SECOND, 128)] * 4 + [sds(LAT_WIRE, 128)] * 2 + [sds(3, ROWS, COLS)],
        smem=1,
        n_any=5,
        scratch=[pltpu.VMEM((LEV, ROWS, COLS), f32)] * 3
        + [
            pltpu.VMEM((OLEV, OROWS, OCOLS), f32),
            pltpu.VMEM((OROWS, OCOLS), jnp.int32),
            pltpu.VMEM((LAT_WIRE, 128), f32),
            pltpu.VMEM((LAT_WIRE, 128), f32),
            pltpu.SemaphoreType.DMA((4, LONS)),
        ],
        cost=cost(5),
        mib=60,
    )(place, tracer, wind_u, wind_v, ocean_temp, land_mask)
    mains, winds, mid = packed[:4], packed[4:8], packed[10]
    pieces = [mains[0]] + [along(mains[s], s) for s in (3, 2, 1)]
    near0, near1 = across(packed[8], packed[9])

    basis = call(basis_kernel, [sds(NLON, NLON, dtype=bf16)] * 2, n_in=4, cost=cost(3))(*wave_tables())
    damp = damp_window(lat_place, polar_rows, ROWS * lat_devices, lat_devices // 8 * ROWS)
    joined = call(
        join_kernel,
        [sds(RIM_WIRE if s in (1, 3) else STRIP_AT, 128) for s in range(LONS)]
        + [sds(WINDOW, 128)]
        + [sds(LAT_WIRE, 128)] * 2,
        smem=1,
        n_in=5,
        scratch=[pltpu.VMEM((WIN, 384), f32)],
        cost=cost(2),
    )(place, near0, near1, mid, ocean_temp, land_mask)
    before, after = joined[5:]
    windows = [joined[4]] + [along(joined[4], s) for s in (3, 2, 1)]
    rims = [joined[0]] + [along(joined[s], s) for s in (3, 2, 1)]
    blows = [winds[0]] + [along(winds[s], s) for s in (3, 2, 1)]

    heat, speed = call(bottom_kernel, [sds(WIN, 384)] * 2, n_in=7, cost=cost(8))(*windows, damp, *basis)
    air_heat, air_speed, air_up, air_down = call(
        pick_kernel, [sds(OROWS, OCOLS)] * 2 + [sds(4, OCOLS)] * 2, smem=1, n_in=4, cost=cost(7),
        scratch=[pltpu.VMEM((4, OCOLS), f32)] * 2,
    )(place, remap_rows, remap_cols, heat, speed)
    air0, air1 = across(air_up, air_down)

    lines = (ROWS + 4) * LB
    far, top, rest = call(
        bulk_kernel,
        [sds(FT, 128)] + [sds(ROWS * LB, NLON, dtype=bf16)] * 2,
        n_in=15,
        n_any=1,
        scratch=[pltpu.VMEM((lines, NLON), f32)] + [pltpu.VMEM((lines - 16, NLON), f32)] * 3,
        cost=cost(13),
        mib=36,
    )(*pieces, *blows, *rims, damp, *basis, air_up)
    far = along(far, 2)
    own, one, three = call(finish_kernel, [sds(FT, 128)] * 3, n_in=4, cost=cost(3))(top, rest, *basis)
    back = [own, along(one, 1), far, along(three, 3)]

    east, west, air_before, air_after = call(
        ring_kernel, [sds(WROWS, 4)] * 2 + [sds(4, OCOLS)] * 2, smem=1, n_in=4, n_any=1, cost=cost(1)
    )(place, air_heat, air_speed, air0, air1, top)
    air_east, air_west = along(east, LONS - 1), along(west, 1)
    ocean_out = call(
        ocean_kernel, sds(OLEV, OROWS, OCOLS), n_in=12, scratch=[pltpu.VMEM((7, WROWS, WCOLS), f32)], cost=cost(3)
    )(
        ocean_temp, land_mask, air_heat, air_speed, before, after, rims[1], rims[3],
        air_before, air_after, air_east, air_west,
    )
    tracer_out = call(unpack_kernel, sds(LEV, ROWS, COLS), smem=1, n_in=4, cost=cost(2))(place, *back)
    return tracer_out, ocean_out


def solution(mesh):
    band = P(None, "lat", "lon")
    cells = P("lat", "lon")
    return jax.shard_map(
        per_device,
        mesh=mesh,
        in_specs=(band, band, band, band, cells, cells, cells, P()),
        out_specs=(band, band),
        check_vma=False,
    )
```

```python
import math

import jax
import jax.numpy as jnp
import numpy as np
from jax import lax
from jax.experimental import pallas as pl
from jax.experimental.pallas import tpu as pltpu
from jax.sharding import PartitionSpec as P


f32 = jnp.float32
bf16 = jnp.bfloat16
LEV, ROWS, COLS, LONS = 32, 24, 288, 4
NLON = COLS * LONS
LB = LEV // LONS
HALF = NLON // 2
OLEV, OROWS, OCOLS = 4, 32, 896
WROWS, WCOLS = 40, 1024
WIN = 32
FT = 54 * 8

advect_coef = 0.2
diffuse_coef = 0.1
flux_coef = 0.25
ocean_diffuse = 0.15
vertical_mix = 0.2


def call(kernel, out_shape, smem=0, n_in=0, n_any=0, out_any=0, n_out=0, scratch=(), cost=None, mib=24, aliases=None):
    specs = [pl.BlockSpec(memory_space=pltpu.SMEM)] * smem + [pl.BlockSpec(memory_space=pltpu.VMEM)] * n_in
    specs += [pl.BlockSpec(memory_space=pl.ANY)] * n_any
    outs = {}
    if out_any:
        spaces = [pl.ANY] * out_any + [pltpu.VMEM] * (n_out - out_any)
        outs["out_specs"] = [pl.BlockSpec(memory_space=space) for space in spaces]
    return pl.pallas_call(
        kernel,
        out_shape=out_shape,
        **outs,
        input_output_aliases=aliases or {},
        in_specs=specs,
        scratch_shapes=scratch,
        cost_estimate=cost,
        compiler_params=pltpu.CompilerParams(vmem_limit_bytes=mib << 20),
    )


def cost(us):
    return pl.CostEstimate(flops=0, transcendentals=0, bytes_accessed=int(us * 3.0e6))


def sds(*shape, dtype=f32):
    return jax.ShapeDtypeStruct(shape, dtype)


LEVEL_AT, OCEAN_AT, SEA_AT, LAT_WIRE = 288, 312, 368, 384
FIRST, SECOND = FT + 192, 2 * FT - 192
STRIP_AT, RIM_WIRE, WINDOW = 144, 184, 216
TILES = OCOLS // 128
THIRD, TABLE = 40, 80


def wire_places(f, first, second):
    if f == 0:
        return ((first, 0), (first, 192), (first, 384))
    if f == 1:
        return ((first, FT), (second, 0), (second, 192))
    return ((second, 240), (second, 432), (second, 624))


def cross(place, a, b, first, second):
    odd = jnp.full(a.shape, place[1] % 2, jnp.int32) == 1
    first[...] = jnp.where(odd, a[...], b[...])
    second[...] = jnp.where(odd, b[...], a[...])


def pack_kernel(
    q_in, u_in, v_in, t_in, mask_in, a0, a1, a2, a3, b0, b1, b2, b3, x0, x1, mid,
    q, u, v, t, mask, up, down, firsts, seconds, sems, out_sems,
):
    place = (lax.axis_index("lon"), lax.axis_index("lat"))
    copies = [
        [
            pltpu.make_async_copy(source.at[pl.ds(LB * i, LB)], target.at[pl.ds(LB * i, LB)], sems.at[f, i])
            for i in range(LONS)
        ]
        for f, (source, target) in enumerate(((q_in, q), (u_in, u), (v_in, v)))
    ]
    copies.append([pltpu.make_async_copy(t_in, t, sems.at[3, 0]), pltpu.make_async_copy(mask_in, mask, sems.at[3, 1])])
    for group in copies:
        for copy in group:
            copy.start()
    sends = []
    for s, (a, b) in enumerate(zip((a0, a1, a2, a3), (b0, b1, b2, b3))):
        sends.append(
            (
                pltpu.make_async_copy(firsts.at[s], a, out_sems.at[0, s]),
                pltpu.make_async_copy(seconds.at[s], b, out_sems.at[1, s]),
            )
        )
    for f, field in enumerate((q, u, v)):
        for copy in copies[f]:
            copy.wait()
        for s in range(LONS):
            places = wire_places(f, firsts.at[s], seconds.at[s])
            first = (place[0] + s) % LONS * LB
            for l in range(LB):
                for c in range(2):
                    wire, base = places[c]
                    wire[pl.ds(base + l, ROWS, stride=8), :] = field[first + l, :, c * 128 : c * 128 + 128]
                wire, base = places[2]
                wire[pl.ds(base + l, 6, stride=8), :] = jnp.concatenate(
                    [field[first + l, 6 * i : 6 * i + 6, 256:288] for i in range(4)], axis=1
                )
            if f > 0:
                sends[s][f - 1].start()
    for copy in copies[3]:
        copy.wait()
    for s in range(LONS):
        first = (place[0] + s) % LONS * LB
        for l in range(LB):
            for out, rows in ((up, (22, 23, 23, 23)), (down, (0, 1, 0, 0))):
                rems = []
                for i, (field, r) in enumerate(zip((q, q, u, v), rows)):
                    for c in range(2):
                        out[pl.ds(s * 72 + c * 32 + i * 8 + l, 1), :] = field[
                            first + l, r : r + 1, c * 128 : c * 128 + 128
                        ]
                    rems.append(field[first + l, r : r + 1, 256:288])
                out[pl.ds(s * 72 + 64 + l, 1), :] = jnp.concatenate(rems, axis=1)
    for out, a, b, o in ((up, ROWS - 3, ROWS - 2, OROWS - 2), (down, 0, 0, 0)):
        for at, field, r, n in ((0, q, a, 3), (3, u, b, 2), (5, v, b, 2)):
            for c in range(2):
                out[LEVEL_AT + 8 * c + at : LEVEL_AT + 8 * c + at + n, :] = field[
                    LEV - 1, r : r + n, c * 128 : c * 128 + 128
                ]
            out[LEVEL_AT + 16 + at : LEVEL_AT + 16 + at + n, 0:32] = field[LEV - 1, r : r + n, 256:288]
        for c in range(TILES):
            for l in range(OLEV):
                out[OCEAN_AT + 8 * c + 2 * l : OCEAN_AT + 8 * c + 2 * l + 2, :] = t[
                    l, o : o + 2, c * 128 : c * 128 + 128
                ]
            out[SEA_AT + 2 * c : SEA_AT + 2 * c + 2, :] = mask[o : o + 2, c * 128 : c * 128 + 128].astype(f32)
    for f, field in enumerate((q, u, v)):
        mid[f, :, :] = field[LEV - 1, :, :]
    cross(place, up, down, x0, x1)
    for pair in sends:
        for copy in pair:
            copy.wait()


def join_kernel(place, x0, x1, t, mask, mid_in, w0, w1, w2, w3, circle, before, after, win, mid, sem):
    copy = pltpu.make_async_copy(mid_in, mid, sem)
    copy.start()
    cross(place, x1, x0, before, after)
    wires = (w0, w1, w2, w3)
    for s, wire in enumerate(wires):
        wire[0:72, :] = before[s * 72 : s * 72 + 72, :]
        wire[72:144, :] = after[s * 72 : s * 72 + 72, :]
    copy.wait()
    for f, (at, n) in enumerate(((0, 3), (3, 2), (5, 2))):
        win[...] = jnp.zeros((WIN, 384), f32)
        win[4 : 4 + ROWS, 0:COLS] = mid[f, :, :]
        for c in range(3):
            rows = LEVEL_AT + 8 * c + at
            width = 128 if c < 2 else 32
            win[4 - n : 4, c * 128 : c * 128 + width] = before[rows : rows + n, 0:width]
            win[4 + ROWS : 4 + ROWS + n, c * 128 : c * 128 + width] = after[rows : rows + n, 0:width]
        rem = jnp.concatenate([win[8 * i : 8 * i + 8, 256:288] for i in range(4)], axis=1)
        circle[f * 72 : f * 72 + 32, :] = win[:, 0:128]
        circle[f * 72 + 32 : f * 72 + 64, :] = win[:, 128:256]
        circle[f * 72 + 64 : f * 72 + 72, :] = rem
    pad = 128 - 2 * (OLEV + 1)
    for wire, col in ((w3, 0), (w1, OCOLS - 2)):
        tile, lane = col // 128, col % 128
        own = [t[l, :, col : col + 2] for l in range(OLEV)] + [mask[:, col : col + 2].astype(f32)]
        wire[STRIP_AT : STRIP_AT + OROWS, :] = jnp.concatenate(own + [jnp.zeros((OROWS, pad), f32)], axis=1)
        wire[STRIP_AT + OROWS : STRIP_AT + WROWS, :] = jnp.zeros((WROWS - OROWS, 128), f32)
        for near, row in ((after, OROWS), (before, WROWS - 2)):
            base = OCEAN_AT + 8 * tile
            far = [near[base + 2 * l : base + 2 * l + 2, lane : lane + 2] for l in range(OLEV)]
            far.append(near[SEA_AT + 2 * tile : SEA_AT + 2 * tile + 2, lane : lane + 2])
            wire[STRIP_AT + row : STRIP_AT + row + 2, :] = jnp.concatenate(far + [jnp.zeros((2, pad), f32)], axis=1)


def unpack_kernel(place, shifts, wires, out, block, sem):
    copies = []
    for n, (s, wire) in enumerate(zip(shifts, wires)):
        for l in range(LB):
            for c in range(2):
                block[n, l, :, c * 128 : c * 128 + 128] = wire[pl.ds(c * 192 + l, ROWS, stride=8), :]
            rem = wire[pl.ds(384 + l, 6, stride=8), :]
            for i in range(4):
                block[n, l, 6 * i : 6 * i + 6, 256:288] = rem[:, 32 * i : 32 * i + 32]
        first = (place[0] + LONS - s) % LONS * LB
        copies.append(pltpu.make_async_copy(block.at[n], out.at[pl.ds(first, LB)], sem.at[n]))
        copies[-1].start()
    for copy in copies:
        copy.wait()


def unpack_first(place, w0, w2, out, block, sem):
    unpack_kernel(place, (0, 2), (w0, w2), out, block, sem)


def unpack_second(place, w1, w3, half, out, block, sem):
    unpack_kernel(place, (1, 3), (w1, w3), out, block, sem)


def wave_tables():
    slots = np.arange(NLON)[None, :]
    wave = np.where(slots <= HALF, slots, slots - HALF)
    coarse = (32 * np.arange(36)[:, None] * wave) % NLON * (2 * np.pi / NLON)
    fine = (np.arange(32)[:, None] * wave) % NLON * (2 * np.pi / NLON)
    with_cos = np.where(slots <= HALF, np.cos(coarse), np.sin(coarse))
    with_sin = np.where(slots <= HALF, -np.sin(coarse), np.cos(coarse))
    return tuple(a.astype(np.float32) for a in (with_cos, with_sin, np.cos(fine), np.sin(fine)))


def basis_kernel(with_cos, with_sin, cosine, sine, hi, lo):
    def body(a, carry):
        row = pl.multiple_of(a * 32, 32)
        for h in (0, 16):
            value = with_cos[pl.ds(a, 1), :] * cosine[h : h + 16, :] + with_sin[pl.ds(a, 1), :] * sine[h : h + 16, :]
            top = value.astype(bf16)
            hi[pl.ds(row + h, 16), :] = top
            lo[pl.ds(row + h, 16), :] = (value - top.astype(f32)).astype(bf16)
        return carry

    lax.fori_loop(0, 36, body, 0)


def split(x):
    top = x.astype(bf16)
    return top, (x - top.astype(f32)).astype(bf16)


def product(x, hi, lo, back=False):
    top, rest = split(x)
    lines = x.shape[0]
    dims = (((1,), (1 if back else 0,)), ((), ()))

    def dot(a, b):
        return lax.dot_general(a, b[...], dims, preferred_element_type=f32)

    both = dot(jnp.concatenate([top, rest], axis=0), hi)
    return both[:lines] + both[lines:] + dot(top, lo)


def advance(q, north, south, u, v):
    east = pltpu.roll(q, NLON - 1, 1)
    west = pltpu.roll(q, 1, 1)
    advect = u * (east - west) + v * (north - south)
    spread = east + west + north + south - 4.0 * q
    return q - advect_coef * advect + diffuse_coef * spread


def bottom_kernel(w0, w1, w2, w3, damp, bh, bl, heat, speed):
    def circle(f):
        base, parts = f * 72, []
        for w in (w0, w1, w2, w3):
            parts += [w[base : base + 32, :], w[base + 32 : base + 64, :]]
            parts.append(
                jnp.concatenate([w[base + 64 : base + 72, 32 * i : 32 * i + 32] for i in range(4)], axis=0)
            )
        return jnp.concatenate(parts, axis=1)

    q, u, v = circle(0), circle(1), circle(2)
    wind = jnp.abs(u) + jnp.abs(v) + 0.5
    for _ in range(2):
        q = advance(q, pltpu.roll(q, WIN - 1, 0), pltpu.roll(q, 1, 0), u, v)
        q = product(product(q, bh, bl) * damp[...], bh, bl, back=True)
    for out, field in ((heat, q), (speed, wind)):
        out[0:WIN, :] = field[:, 0:128]
        out[WIN : 2 * WIN, :] = field[:, 128:256]
        ends = jnp.concatenate(
            [field[:, 256 : COLS + 1], field[:, NLON - 1 : NLON], jnp.zeros((WIN, THIRD - 34), f32)], axis=1
        )
        out[2 * WIN : 2 * WIN + 9, :] = jnp.concatenate(
            [ends[3 + 9 * i : 12 + 9 * i, :] for i in range(3)] + [jnp.zeros((9, 128 - 3 * THIRD), f32)], axis=1
        )
        out[2 * WIN + 9 : TABLE, :] = jnp.zeros((TABLE - 2 * WIN - 9, 128), f32)


def bulk_kernel(m0, m1, m2, m3, n0, n1, n2, n3, h0, h1, h2, h3, damp, bh, bl, after, far, top_out, rest_out, qs, us, vs, xs):
    halos = (h0, h1, h2, h3)

    def main_slab(f, r):
        parts = []
        for first, second in zip((m0, m1, m2, m3), (n0, n1, n2, n3)):
            (w0, at0), (w1, at1), (w2, at2) = wire_places(f, first, second)
            g, i = r % 6, r // 6
            parts.append(w0[at0 + r * 8 : at0 + r * 8 + 8, :])
            parts.append(w1[at1 + r * 8 : at1 + r * 8 + 8, :])
            parts.append(w2[at2 + g * 8 : at2 + g * 8 + 8, 32 * i : 32 * i + 32])
        return jnp.concatenate(parts, axis=1)

    def halo_slab(side, i):
        parts = []
        for h in halos:
            base = side * 72
            parts.append(h[base + i * 8 : base + i * 8 + 8, :])
            parts.append(h[base + 32 + i * 8 : base + 40 + i * 8, :])
            parts.append(h[base + 64 : base + 72, 32 * i : 32 * i + 32])
        return jnp.concatenate(parts, axis=1)

    def put(ref, slot, value):
        ref[slot * 8 : slot * 8 + 8, :] = value

    for r in range(ROWS):
        put(qs, r + 2, main_slab(0, r))
        put(us, r + 1, main_slab(1, r))
        put(vs, r + 1, main_slab(2, r))
    put(qs, 0, halo_slab(0, 0))
    put(qs, 1, halo_slab(0, 1))
    put(us, 0, halo_slab(0, 2))
    put(vs, 0, halo_slab(0, 3))
    put(qs, 26, halo_slab(1, 0))
    put(qs, 27, halo_slab(1, 1))
    put(us, 25, halo_slab(1, 2))
    put(vs, 25, halo_slab(1, 3))

    def at(ref, slot):
        return ref[pl.ds(pl.multiple_of(slot * 8, 8), 8), :]

    def scale(count, first):
        def body(r, carry):
            xs[pl.ds(pl.multiple_of(r * 8, 8), 8), :] = at(xs, r) * damp[pl.ds(r + first, 1), :]
            return carry

        lax.fori_loop(0, count, body, 0)

    def first(r, carry):
        xs[pl.ds(pl.multiple_of(r * 8, 8), 8), :] = advance(
            at(qs, r + 1), at(qs, r + 2), at(qs, r), at(us, r), at(vs, r)
        )
        return carry

    lax.fori_loop(0, ROWS + 2, first, 0)
    xs[...] = product(xs[...], bh, bl)
    scale(ROWS + 2, 3)
    qs[0:208, :] = product(xs[...], bh, bl, back=True)

    def second(r, carry):
        xs[pl.ds(pl.multiple_of(r * 8, 8), 8), :] = advance(
            at(qs, r + 1), at(qs, r + 2), at(qs, r), at(us, r + 1), at(vs, r + 1)
        )
        return carry

    lax.fori_loop(0, ROWS, second, 0)
    xs[0:192, :] = product(xs[0:192, :], bh, bl)
    scale(ROWS, 4)
    top, rest = split(xs[0:192, :])
    top_out[...] = top
    rest_out[...] = rest
    write_piece(far, project(top, rest, bh[2 * COLS : 3 * COLS, :], bl[2 * COLS : 3 * COLS, :]))


def project(top, rest, hi, lo):
    dims = (((1,), (1,)), ((), ()))
    lines = top.shape[0]
    both = lax.dot_general(jnp.concatenate([top, rest], axis=0), hi, dims, preferred_element_type=f32)
    return both[:lines] + both[lines:] + lax.dot_general(top, lo, dims, preferred_element_type=f32)


def write_piece(out, piece):
    for g in range(6):
        rems = []
        for r in range(g, ROWS, 6):
            out[r * 8 : r * 8 + 8, :] = piece[r * 8 : r * 8 + 8, 0:128]
            out[192 + r * 8 : 200 + r * 8, :] = piece[r * 8 : r * 8 + 8, 128:256]
            rems.append(piece[r * 8 : r * 8 + 8, 256:288])
        out[384 + g * 8 : 392 + g * 8, :] = jnp.concatenate(rems, axis=1)


def finish_kernel(top, rest, bh, bl, o1, o3):
    for out, p in ((o3, 3), (o1, 1)):
        rows = slice(p * COLS, p * COLS + COLS)
        write_piece(out, project(top[...], rest[...], bh[rows, :], bl[rows, :]))


def own_kernel(top, rest, bh, bl, behind, out):
    write_piece(out, project(top[...], rest[...], bh[0:COLS, :], bl[0:COLS, :]))


def pick_kernel(place, rows, cols, heat, speed, air_heat, air_speed, x0, x1, up, down):
    def body(k, carry):
        start = pl.multiple_of(k * 8, 8)
        for c in range(TILES):
            row = rows[pl.ds(start, 8), c * 128 : c * 128 + 128] - place[1] * ROWS + 4
            col = cols[pl.ds(start, 8), c * 128 : c * 128 + 128] - place[0] * COLS
            col = jnp.where(col < 0, col + NLON, col)
            part = jnp.where(row >= 21, 2, jnp.where(row >= 12, 1, 0))
            end = jnp.where(col > COLS, 33, col - 256)
            last = col >= 256
            key = jnp.where(last, 2 * WIN - 3 + row - 9 * part, row + WIN * (col >> 7))
            lane = jnp.where(last, end + THIRD * part, col & 127)
            got_heat = jnp.zeros((8, 128), f32)
            got_speed = jnp.zeros((8, 128), f32)
            for n in (*range(3, 29), *range(WIN + 3, WIN + 29), *range(2 * WIN, 2 * WIN + 9)):
                mine = key == n
                line_heat = jnp.broadcast_to(heat[n : n + 1, :], (8, 128))
                line_speed = jnp.broadcast_to(speed[n : n + 1, :], (8, 128))
                got_heat = jnp.where(mine, jnp.take_along_axis(line_heat, lane, axis=1), got_heat)
                got_speed = jnp.where(mine, jnp.take_along_axis(line_speed, lane, axis=1), got_speed)
            air_heat[pl.ds(start, 8), c * 128 : c * 128 + 128] = got_heat
            air_speed[pl.ds(start, 8), c * 128 : c * 128 + 128] = got_speed
        return carry

    lax.fori_loop(0, OROWS // 8, body, 0)
    for f, field in enumerate((air_heat, air_speed)):
        up[2 * f : 2 * f + 2, :] = field[OROWS - 2 : OROWS, :]
        down[2 * f : 2 * f + 2, :] = field[0:2, :]
    cross(place, up, down, x0, x1)


def ring_kernel(place, heat, speed, x0, x1, behind, east, west, before, after):
    cross(place, x1, x0, before, after)
    for out, col in ((east, 0), (west, OCOLS - 2)):
        out[0:OROWS, :] = jnp.concatenate([heat[:, col : col + 2], speed[:, col : col + 2]], axis=1)
        out[OROWS:WROWS, :] = jnp.zeros((WROWS - OROWS, 4), f32)
        for near, row in ((after, OROWS), (before, WROWS - 2)):
            out[row : row + 2, :] = jnp.concatenate([near[0:2, col : col + 2], near[2:4, col : col + 2]], axis=1)


def ocean_kernel(t, mask, heat, speed, before, after, east, west, air_before, air_after, air_east, air_west, out, win):
    gap = jnp.zeros((WROWS, 124), f32)
    strip = slice(STRIP_AT, STRIP_AT + WROWS)

    def window(field, slot, above, below, right, left):
        win[slot, OROWS:WROWS, :] = jnp.zeros((WROWS - OROWS, WCOLS), f32)
        win[slot, 0:OROWS, 0:OCOLS] = field
        for c in range(TILES):
            win[slot, OROWS : OROWS + 2, c * 128 : c * 128 + 128] = below(c)
            win[slot, WROWS - 2 : WROWS, c * 128 : c * 128 + 128] = above(c)
        win[slot, :, OCOLS:WCOLS] = jnp.concatenate([right, gap, left], axis=1)
        return win[slot]

    def sea_rows(wire):
        return lambda c: wire[SEA_AT + 2 * c : SEA_AT + 2 * c + 2, :]

    def level_rows(wire, l):
        return lambda c: wire[OCEAN_AT + 8 * c + 2 * l : OCEAN_AT + 8 * c + 2 * l + 2, :]

    def air_rows(wire, f):
        return lambda c: wire[2 * f : 2 * f + 2, c * 128 : c * 128 + 128]

    temps = [
        window(
            t[l], l, level_rows(before, l), level_rows(after, l),
            east[strip, 2 * l : 2 * l + 2], west[strip, 2 * l : 2 * l + 2],
        )
        for l in range(OLEV)
    ]
    sea = window(mask[...].astype(f32), 4, sea_rows(before), sea_rows(after), east[strip, 8:10], west[strip, 8:10])
    air = [
        window(
            field[...], 5 + f, air_rows(air_before, f), air_rows(air_after, f),
            air_east[:, 2 * f : 2 * f + 2], air_west[:, 2 * f : 2 * f + 2],
        )
        for f, field in enumerate((heat, speed))
    ]

    def beside(field):
        return (
            pltpu.roll(field, WCOLS - 1, 1),
            pltpu.roll(field, 1, 1),
            pltpu.roll(field, WROWS - 1, 0),
            pltpu.roll(field, 1, 0),
        )

    seas = beside(sea)
    rate = sea * flux_coef * air[1]
    for _ in range(2):
        temps[0] = temps[0] + rate * (air[0] - temps[0])
        moved = []
        for field in temps:
            total = jnp.zeros_like(field)
            for near_sea, near in zip(seas, beside(field)):
                total = total + near_sea * (near - field)
            moved.append(field + ocean_diffuse * (sea * total))
        temps = [
            moved[l]
            + vertical_mix * sea * (moved[max(l - 1, 0)] + moved[min(l + 1, OLEV - 1)] - 2.0 * moved[l])
            for l in range(OLEV)
        ]
    for l in range(OLEV):
        out[l, :, :] = temps[l][0:OROWS, 0:OCOLS]


def damp_window(lat_place, polar_rows, lat_total, band_rows):
    slots = np.arange(NLON)
    waves = np.where(slots < HALF, slots, np.where(slots == HALF, HALF, slots - HALF))
    weight = np.where((slots == 0) | (slots == HALF), 1.0, 2.0) / NLON
    sine = np.where(waves > 0, np.sin(np.pi * waves / NLON), 1.0)
    row_index = lat_place * ROWS - 4 + jnp.arange(WIN, dtype=jnp.int32)
    latitude_cos = jnp.sin(math.pi * (row_index.astype(f32) + 0.5) / lat_total)
    ratio = latitude_cos / math.sin(math.pi * band_rows / lat_total)
    damping = jnp.minimum(1.0, ratio[:, None] / sine.astype(np.float32)[None, :])
    damping = jnp.where(waves[None, :] > 0, damping, 1.0)
    listed = jnp.any(row_index[:, None] == polar_rows[None, :], axis=1)
    inside = (row_index >= 0) & (row_index < lat_total)
    table = jnp.where(listed[:, None], damping, 1.0) * weight.astype(np.float32)[None, :]
    return jnp.where(inside[:, None], table, 0.0)


def per_device(tracer, wind_u, wind_v, ocean_temp, land_mask, remap_rows, remap_cols, polar_rows):
    lat_devices = lax.axis_size("lat")
    lat_place, lon_place = lax.axis_index("lat"), lax.axis_index("lon")
    place = jnp.stack([lon_place, lat_place]).astype(jnp.int32)
    swaps = [
        [pair for i in range(start, lat_devices - 1, 2) for pair in ((i, i + 1), (i + 1, i))] for start in (1, 0)
    ]

    def along(x, s):
        return lax.ppermute(x, "lon", [(i, (i + s) % LONS) for i in range(LONS)])

    def across(first, second):
        got = lax.ppermute(first, "lat", swaps[0])
        return got, lax.ppermute(second, "lat", swaps[1])

    packed = call(
        pack_kernel,
        [sds(FIRST, 128)] * 4 + [sds(SECOND, 128)] * 4 + [sds(LAT_WIRE, 128)] * 2 + [sds(3, ROWS, COLS)],
        n_any=5,
        out_any=8,
        n_out=11,
        scratch=[pltpu.VMEM((LEV, ROWS, COLS), f32)] * 3
        + [
            pltpu.VMEM((OLEV, OROWS, OCOLS), f32),
            pltpu.VMEM((OROWS, OCOLS), jnp.int32),
            pltpu.VMEM((LAT_WIRE, 128), f32),
            pltpu.VMEM((LAT_WIRE, 128), f32),
            pltpu.VMEM((LONS, FIRST, 128), f32),
            pltpu.VMEM((LONS, SECOND, 128), f32),
            pltpu.SemaphoreType.DMA((4, LONS)),
            pltpu.SemaphoreType.DMA((2, LONS)),
        ],
        cost=cost(5),
        mib=60,
    )(tracer, wind_u, wind_v, ocean_temp, land_mask)
    mains, winds, mid = packed[:4], packed[4:8], packed[10]
    pieces = [mains[0]] + [along(mains[s], s) for s in (3, 2, 1)]
    near0, near1 = across(packed[8], packed[9])

    basis = call(basis_kernel, [sds(NLON, NLON, dtype=bf16)] * 2, n_in=4, cost=cost(3))(*wave_tables())
    damp = damp_window(lat_place, polar_rows, ROWS * lat_devices, lat_devices // 8 * ROWS)
    joined = call(
        join_kernel,
        [sds(RIM_WIRE if s in (1, 3) else STRIP_AT, 128) for s in range(LONS)]
        + [sds(WINDOW, 128)]
        + [sds(LAT_WIRE, 128)] * 2,
        smem=1,
        n_in=4,
        n_any=1,
        scratch=[pltpu.VMEM((WIN, 384), f32), pltpu.VMEM((3, ROWS, COLS), f32), pltpu.SemaphoreType.DMA],
        cost=cost(2),
    )(place, near0, near1, ocean_temp, land_mask, mid)
    before, after = joined[5:]
    windows = [joined[4]] + [along(joined[4], s) for s in (3, 2, 1)]
    rims = [joined[0]] + [along(joined[s], s) for s in (3, 2, 1)]
    blows = [winds[0]] + [along(winds[s], s) for s in (3, 2, 1)]

    heat, speed = call(bottom_kernel, [sds(TABLE, 128)] * 2, n_in=7, cost=cost(8))(*windows, damp, *basis)
    air_heat, air_speed, air_up, air_down = call(
        pick_kernel, [sds(OROWS, OCOLS)] * 2 + [sds(4, OCOLS)] * 2, smem=1, n_in=4, cost=cost(7),
        scratch=[pltpu.VMEM((4, OCOLS), f32)] * 2,
    )(place, remap_rows, remap_cols, heat, speed)
    air0, air1 = across(air_up, air_down)

    lines = (ROWS + 4) * LB
    far, top, rest = call(
        bulk_kernel,
        [sds(FT, 128)] + [sds(ROWS * LB, NLON, dtype=bf16)] * 2,
        n_in=15,
        n_any=1,
        scratch=[pltpu.VMEM((lines, NLON), f32)] + [pltpu.VMEM((lines - 16, NLON), f32)] * 3,
        cost=cost(13),
        mib=36,
    )(*pieces, *blows, *rims, damp, *basis, air_up)
    far = along(far, 2)
    one, three = call(finish_kernel, [sds(FT, 128)] * 2, n_in=4, cost=cost(2))(top, rest, *basis)
    own = call(own_kernel, sds(FT, 128), n_in=4, n_any=1, cost=cost(1))(top, rest, *basis, one)
    back = [own, along(one, 1), far, along(three, 3)]

    east, west, air_before, air_after = call(
        ring_kernel, [sds(WROWS, 4)] * 2 + [sds(4, OCOLS)] * 2, smem=1, n_in=4, n_any=1, cost=cost(1)
    )(place, air_heat, air_speed, air0, air1, top)
    air_east, air_west = along(east, LONS - 1), along(west, 1)
    ocean_out = call(
        ocean_kernel, sds(OLEV, OROWS, OCOLS), n_in=12, scratch=[pltpu.VMEM((7, WROWS, WCOLS), f32)], cost=cost(3)
    )(
        ocean_temp, land_mask, air_heat, air_speed, before, after, rims[1], rims[3],
        air_before, air_after, air_east, air_west,
    )
    scratch = [pltpu.VMEM((2, LB, ROWS, COLS), f32), pltpu.SemaphoreType.DMA((2,))]
    half = call(
        unpack_first, [sds(LEV, ROWS, COLS)], smem=1, n_in=2, out_any=1, n_out=1, scratch=scratch, cost=cost(1)
    )(place, back[0], back[2])[0]
    tracer_out = call(
        unpack_second, [sds(LEV, ROWS, COLS)], smem=1, n_in=2, n_any=1, out_any=1, n_out=1, scratch=scratch,
        cost=cost(1), aliases={3: 0},
    )(place, back[1], back[3], half)[0]
    return tracer_out, ocean_out


def solution(mesh):
    band = P(None, "lat", "lon")
    cells = P("lat", "lon")
    return jax.shard_map(
        per_device,
        mesh=mesh,
        in_specs=(band, band, band, band, cells, cells, cells, P()),
        out_specs=(band, band),
        check_vma=False,
    )
```

```python
import math

import jax
import jax.numpy as jnp
import numpy as np
from jax import lax
from jax.experimental import pallas as pl
from jax.experimental.pallas import tpu as pltpu
from jax.sharding import PartitionSpec as P


f32 = jnp.float32
bf16 = jnp.bfloat16
LEV, ROWS, COLS, LONS = 32, 24, 288, 4
NLON = COLS * LONS
LB = LEV // LONS
HALF = NLON // 2
OLEV, OROWS, OCOLS = 4, 32, 896
WROWS, WCOLS = 40, 1024
WIN = 32
FT = 54 * 8

advect_coef = 0.2
diffuse_coef = 0.1
flux_coef = 0.25
ocean_diffuse = 0.15
vertical_mix = 0.2


def call(kernel, out_shape, smem=0, n_in=0, n_any=0, out_any=0, n_out=0, scratch=(), cost=None, mib=24, aliases=None):
    specs = [pl.BlockSpec(memory_space=pltpu.SMEM)] * smem + [pl.BlockSpec(memory_space=pltpu.VMEM)] * n_in
    specs += [pl.BlockSpec(memory_space=pl.ANY)] * n_any
    outs = {}
    if out_any:
        spaces = [pl.ANY] * out_any + [pltpu.VMEM] * (n_out - out_any)
        outs["out_specs"] = [pl.BlockSpec(memory_space=space) for space in spaces]
    return pl.pallas_call(
        kernel,
        out_shape=out_shape,
        **outs,
        input_output_aliases=aliases or {},
        in_specs=specs,
        scratch_shapes=scratch,
        cost_estimate=cost,
        compiler_params=pltpu.CompilerParams(vmem_limit_bytes=mib << 20),
    )


def cost(us):
    return pl.CostEstimate(flops=0, transcendentals=0, bytes_accessed=int(us * 3.0e6))


def sds(*shape, dtype=f32):
    return jax.ShapeDtypeStruct(shape, dtype)


LEVEL_AT, OCEAN_AT, SEA_AT, LAT_WIRE = 288, 312, 368, 384
FIRST, SECOND = FT + 240, 2 * FT - 240
STRIP_AT, RIM_WIRE, WINDOW = 144, 184, 216
TILES = OCOLS // 128
THIRD, TABLE = 40, 80


def wire_places(f, first, second):
    if f == 0:
        return ((first, 0), (first, 192), (first, 384))
    if f == 1:
        return ((first, FT), (second, 0), (first, FT + 192))
    return ((second, 192), (second, 384), (second, 576))


def cross(place, a, b, first, second):
    odd = jnp.full(a.shape, place[1] % 2, jnp.int32) == 1
    first[...] = jnp.where(odd, a[...], b[...])
    second[...] = jnp.where(odd, b[...], a[...])


def pack_kernel(
    q_in, u_in, v_in, t_in, mask_in, a0, a1, a2, a3, b0, b1, b2, b3, x0, x1, mid,
    q, u, v, t, mask, up, down, firsts, seconds, sems, out_sems,
):
    place = (lax.axis_index("lon"), lax.axis_index("lat"))
    copies = [
        [
            pltpu.make_async_copy(source.at[pl.ds(LB * i, LB)], target.at[pl.ds(LB * i, LB)], sems.at[f, i])
            for i in range(LONS)
        ]
        for f, (source, target) in enumerate(((q_in, q), (u_in, u), (v_in, v)))
    ]
    copies.append([pltpu.make_async_copy(t_in, t, sems.at[3, 0]), pltpu.make_async_copy(mask_in, mask, sems.at[3, 1])])
    for group in copies:
        for copy in group:
            copy.start()
    sends = []
    for s, (a, b) in enumerate(zip((a0, a1, a2, a3), (b0, b1, b2, b3))):
        sends.append(
            (
                pltpu.make_async_copy(firsts.at[s], a, out_sems.at[0, s]),
                pltpu.make_async_copy(seconds.at[s], b, out_sems.at[1, s]),
            )
        )
    for f, field in enumerate((q, u, v)):
        for copy in copies[f]:
            copy.wait()
        for s in range(LONS):
            places = wire_places(f, firsts.at[s], seconds.at[s])
            first = (place[0] + s) % LONS * LB
            for l in range(LB):
                for c in range(2):
                    wire, base = places[c]
                    wire[pl.ds(base + l, ROWS, stride=8), :] = field[first + l, :, c * 128 : c * 128 + 128]
                wire, base = places[2]
                wire[pl.ds(base + l, 6, stride=8), :] = jnp.concatenate(
                    [field[first + l, 6 * i : 6 * i + 6, 256:288] for i in range(4)], axis=1
                )
            if f > 0:
                sends[s][f - 1].start()
    for copy in copies[3]:
        copy.wait()
    for s in range(LONS):
        first = (place[0] + s) % LONS * LB
        for l in range(LB):
            for out, rows in ((up, (22, 23, 23, 23)), (down, (0, 1, 0, 0))):
                rems = []
                for i, (field, r) in enumerate(zip((q, q, u, v), rows)):
                    for c in range(2):
                        out[pl.ds(s * 72 + c * 32 + i * 8 + l, 1), :] = field[
                            first + l, r : r + 1, c * 128 : c * 128 + 128
                        ]
                    rems.append(field[first + l, r : r + 1, 256:288])
                out[pl.ds(s * 72 + 64 + l, 1), :] = jnp.concatenate(rems, axis=1)
    for out, a, b, o in ((up, ROWS - 3, ROWS - 2, OROWS - 2), (down, 0, 0, 0)):
        for at, field, r, n in ((0, q, a, 3), (3, u, b, 2), (5, v, b, 2)):
            for c in range(2):
                out[LEVEL_AT + 8 * c + at : LEVEL_AT + 8 * c + at + n, :] = field[
                    LEV - 1, r : r + n, c * 128 : c * 128 + 128
                ]
            out[LEVEL_AT + 16 + at : LEVEL_AT + 16 + at + n, 0:32] = field[LEV - 1, r : r + n, 256:288]
        for c in range(TILES):
            for l in range(OLEV):
                out[OCEAN_AT + 8 * c + 2 * l : OCEAN_AT + 8 * c + 2 * l + 2, :] = t[
                    l, o : o + 2, c * 128 : c * 128 + 128
                ]
            out[SEA_AT + 2 * c : SEA_AT + 2 * c + 2, :] = mask[o : o + 2, c * 128 : c * 128 + 128].astype(f32)
    for f, field in enumerate((q, u, v)):
        mid[f, :, :] = field[LEV - 1, :, :]
    cross(place, up, down, x0, x1)
    for pair in sends:
        for copy in pair:
            copy.wait()


def join_kernel(place, x0, x1, t, mask, mid_in, w0, w1, w2, w3, circle, before, after, win, mid, sem):
    copy = pltpu.make_async_copy(mid_in, mid, sem)
    copy.start()
    cross(place, x1, x0, before, after)
    wires = (w0, w1, w2, w3)
    for s, wire in enumerate(wires):
        wire[0:72, :] = before[s * 72 : s * 72 + 72, :]
        wire[72:144, :] = after[s * 72 : s * 72 + 72, :]
    copy.wait()
    for f, (at, n) in enumerate(((0, 3), (3, 2), (5, 2))):
        win[...] = jnp.zeros((WIN, 384), f32)
        win[4 : 4 + ROWS, 0:COLS] = mid[f, :, :]
        for c in range(3):
            rows = LEVEL_AT + 8 * c + at
            width = 128 if c < 2 else 32
            win[4 - n : 4, c * 128 : c * 128 + width] = before[rows : rows + n, 0:width]
            win[4 + ROWS : 4 + ROWS + n, c * 128 : c * 128 + width] = after[rows : rows + n, 0:width]
        rem = jnp.concatenate([win[8 * i : 8 * i + 8, 256:288] for i in range(4)], axis=1)
        circle[f * 72 : f * 72 + 32, :] = win[:, 0:128]
        circle[f * 72 + 32 : f * 72 + 64, :] = win[:, 128:256]
        circle[f * 72 + 64 : f * 72 + 72, :] = rem
    pad = 128 - 2 * (OLEV + 1)
    for wire, col in ((w3, 0), (w1, OCOLS - 2)):
        tile, lane = col // 128, col % 128
        own = [t[l, :, col : col + 2] for l in range(OLEV)] + [mask[:, col : col + 2].astype(f32)]
        wire[STRIP_AT : STRIP_AT + OROWS, :] = jnp.concatenate(own + [jnp.zeros((OROWS, pad), f32)], axis=1)
        wire[STRIP_AT + OROWS : STRIP_AT + WROWS, :] = jnp.zeros((WROWS - OROWS, 128), f32)
        for near, row in ((after, OROWS), (before, WROWS - 2)):
            base = OCEAN_AT + 8 * tile
            far = [near[base + 2 * l : base + 2 * l + 2, lane : lane + 2] for l in range(OLEV)]
            far.append(near[SEA_AT + 2 * tile : SEA_AT + 2 * tile + 2, lane : lane + 2])
            wire[STRIP_AT + row : STRIP_AT + row + 2, :] = jnp.concatenate(far + [jnp.zeros((2, pad), f32)], axis=1)


def unpack_kernel(place, shifts, wires, out, block, sem):
    copies = []
    for n, (s, wire) in enumerate(zip(shifts, wires)):
        for l in range(LB):
            for c in range(2):
                block[n, l, :, c * 128 : c * 128 + 128] = wire[pl.ds(c * 192 + l, ROWS, stride=8), :]
            rem = wire[pl.ds(384 + l, 6, stride=8), :]
            for i in range(4):
                block[n, l, 6 * i : 6 * i + 6, 256:288] = rem[:, 32 * i : 32 * i + 32]
        first = (place[0] + LONS - s) % LONS * LB
        copies.append(pltpu.make_async_copy(block.at[n], out.at[pl.ds(first, LB)], sem.at[n]))
        copies[-1].start()
    for copy in copies:
        copy.wait()


def unpack_first(place, w0, w2, out, block, sem):
    unpack_kernel(place, (0, 2), (w0, w2), out, block, sem)


def unpack_second(place, w1, w3, half, out, block, sem):
    unpack_kernel(place, (1, 3), (w1, w3), out, block, sem)


def wave_tables():
    slots = np.arange(NLON)[None, :]
    wave = np.where(slots <= HALF, slots, slots - HALF)
    coarse = (32 * np.arange(36)[:, None] * wave) % NLON * (2 * np.pi / NLON)
    fine = (np.arange(32)[:, None] * wave) % NLON * (2 * np.pi / NLON)
    with_cos = np.where(slots <= HALF, np.cos(coarse), np.sin(coarse))
    with_sin = np.where(slots <= HALF, -np.sin(coarse), np.cos(coarse))
    return tuple(a.astype(np.float32) for a in (with_cos, with_sin, np.cos(fine), np.sin(fine)))


def basis_kernel(with_cos, with_sin, cosine, sine, hi, lo):
    def body(a, carry):
        row = pl.multiple_of(a * 32, 32)
        for h in (0, 16):
            value = with_cos[pl.ds(a, 1), :] * cosine[h : h + 16, :] + with_sin[pl.ds(a, 1), :] * sine[h : h + 16, :]
            top = value.astype(bf16)
            hi[pl.ds(row + h, 16), :] = top
            lo[pl.ds(row + h, 16), :] = (value - top.astype(f32)).astype(bf16)
        return carry

    lax.fori_loop(0, 36, body, 0)


def split(x):
    top = x.astype(bf16)
    return top, (x - top.astype(f32)).astype(bf16)


def product(x, hi, lo, back=False):
    top, rest = split(x)
    lines = x.shape[0]
    dims = (((1,), (1 if back else 0,)), ((), ()))

    def dot(a, b):
        return lax.dot_general(a, b[...], dims, preferred_element_type=f32)

    both = dot(jnp.concatenate([top, rest], axis=0), hi)
    return both[:lines] + both[lines:] + dot(top, lo)


def advance(q, north, south, u, v):
    east = pltpu.roll(q, NLON - 1, 1)
    west = pltpu.roll(q, 1, 1)
    advect = u * (east - west) + v * (north - south)
    spread = east + west + north + south - 4.0 * q
    return q - advect_coef * advect + diffuse_coef * spread


def bottom_kernel(w0, w1, w2, w3, damp, bh, bl, heat, speed):
    def circle(f):
        base, parts = f * 72, []
        for w in (w0, w1, w2, w3):
            parts += [w[base : base + 32, :], w[base + 32 : base + 64, :]]
            parts.append(
                jnp.concatenate([w[base + 64 : base + 72, 32 * i : 32 * i + 32] for i in range(4)], axis=0)
            )
        return jnp.concatenate(parts, axis=1)

    q, u, v = circle(0), circle(1), circle(2)
    wind = jnp.abs(u) + jnp.abs(v) + 0.5
    for _ in range(2):
        q = advance(q, pltpu.roll(q, WIN - 1, 0), pltpu.roll(q, 1, 0), u, v)
        q = product(product(q, bh, bl) * damp[...], bh, bl, back=True)
    for out, field in ((heat, q), (speed, wind)):
        out[0:WIN, :] = field[:, 0:128]
        out[WIN : 2 * WIN, :] = field[:, 128:256]
        ends = jnp.concatenate(
            [field[:, 256 : COLS + 1], field[:, NLON - 1 : NLON], jnp.zeros((WIN, THIRD - 34), f32)], axis=1
        )
        out[2 * WIN : 2 * WIN + 9, :] = jnp.concatenate(
            [ends[3 + 9 * i : 12 + 9 * i, :] for i in range(3)] + [jnp.zeros((9, 128 - 3 * THIRD), f32)], axis=1
        )
        out[2 * WIN + 9 : TABLE, :] = jnp.zeros((TABLE - 2 * WIN - 9, 128), f32)


def bulk_kernel(m0, m1, m2, m3, n0, n1, n2, n3, h0, h1, h2, h3, damp, bh, bl, after, far, top_out, rest_out, qs, us, vs, xs):
    halos = (h0, h1, h2, h3)

    def main_slab(f, r):
        parts = []
        for first, second in zip((m0, m1, m2, m3), (n0, n1, n2, n3)):
            (w0, at0), (w1, at1), (w2, at2) = wire_places(f, first, second)
            g, i = r % 6, r // 6
            parts.append(w0[at0 + r * 8 : at0 + r * 8 + 8, :])
            parts.append(w1[at1 + r * 8 : at1 + r * 8 + 8, :])
            parts.append(w2[at2 + g * 8 : at2 + g * 8 + 8, 32 * i : 32 * i + 32])
        return jnp.concatenate(parts, axis=1)

    def halo_slab(side, i):
        parts = []
        for h in halos:
            base = side * 72
            parts.append(h[base + i * 8 : base + i * 8 + 8, :])
            parts.append(h[base + 32 + i * 8 : base + 40 + i * 8, :])
            parts.append(h[base + 64 : base + 72, 32 * i : 32 * i + 32])
        return jnp.concatenate(parts, axis=1)

    def put(ref, slot, value):
        ref[slot * 8 : slot * 8 + 8, :] = value

    for r in range(ROWS):
        put(qs, r + 2, main_slab(0, r))
        put(us, r + 1, main_slab(1, r))
        put(vs, r + 1, main_slab(2, r))
    put(qs, 0, halo_slab(0, 0))
    put(qs, 1, halo_slab(0, 1))
    put(us, 0, halo_slab(0, 2))
    put(vs, 0, halo_slab(0, 3))
    put(qs, 26, halo_slab(1, 0))
    put(qs, 27, halo_slab(1, 1))
    put(us, 25, halo_slab(1, 2))
    put(vs, 25, halo_slab(1, 3))

    def at(ref, slot):
        return ref[pl.ds(pl.multiple_of(slot * 8, 8), 8), :]

    def scale(count, first):
        def body(r, carry):
            xs[pl.ds(pl.multiple_of(r * 8, 8), 8), :] = at(xs, r) * damp[pl.ds(r + first, 1), :]
            return carry

        lax.fori_loop(0, count, body, 0)

    def first(r, carry):
        xs[pl.ds(pl.multiple_of(r * 8, 8), 8), :] = advance(
            at(qs, r + 1), at(qs, r + 2), at(qs, r), at(us, r), at(vs, r)
        )
        return carry

    lax.fori_loop(0, ROWS + 2, first, 0)
    xs[...] = product(xs[...], bh, bl)
    scale(ROWS + 2, 3)
    qs[0:208, :] = product(xs[...], bh, bl, back=True)

    def second(r, carry):
        xs[pl.ds(pl.multiple_of(r * 8, 8), 8), :] = advance(
            at(qs, r + 1), at(qs, r + 2), at(qs, r), at(us, r + 1), at(vs, r + 1)
        )
        return carry

    lax.fori_loop(0, ROWS, second, 0)
    xs[0:192, :] = product(xs[0:192, :], bh, bl)
    scale(ROWS, 4)
    top, rest = split(xs[0:192, :])
    top_out[...] = top
    rest_out[...] = rest
    write_piece(far, project(top, rest, bh[2 * COLS : 3 * COLS, :], bl[2 * COLS : 3 * COLS, :]))


def project(top, rest, hi, lo):
    dims = (((1,), (1,)), ((), ()))
    lines = top.shape[0]
    both = lax.dot_general(jnp.concatenate([top, rest], axis=0), hi, dims, preferred_element_type=f32)
    return both[:lines] + both[lines:] + lax.dot_general(top, lo, dims, preferred_element_type=f32)


def write_piece(out, piece):
    for g in range(6):
        rems = []
        for r in range(g, ROWS, 6):
            out[r * 8 : r * 8 + 8, :] = piece[r * 8 : r * 8 + 8, 0:128]
            out[192 + r * 8 : 200 + r * 8, :] = piece[r * 8 : r * 8 + 8, 128:256]
            rems.append(piece[r * 8 : r * 8 + 8, 256:288])
        out[384 + g * 8 : 392 + g * 8, :] = jnp.concatenate(rems, axis=1)


def finish_kernel(top, rest, bh, bl, o1, o3):
    for out, p in ((o3, 3), (o1, 1)):
        rows = slice(p * COLS, p * COLS + COLS)
        write_piece(out, project(top[...], rest[...], bh[rows, :], bl[rows, :]))


def own_kernel(top, rest, bh, bl, behind, out):
    write_piece(out, project(top[...], rest[...], bh[0:COLS, :], bl[0:COLS, :]))


def pick_kernel(place, rows, cols, heat, speed, air_heat, air_speed, x0, x1, up, down):
    def body(k, carry):
        start = pl.multiple_of(k * 8, 8)
        for c in range(TILES):
            row = rows[pl.ds(start, 8), c * 128 : c * 128 + 128] - place[1] * ROWS + 4
            col = cols[pl.ds(start, 8), c * 128 : c * 128 + 128] - place[0] * COLS
            col = jnp.where(col < 0, col + NLON, col)
            part = jnp.where(row >= 21, 2, jnp.where(row >= 12, 1, 0))
            end = jnp.where(col > COLS, 33, col - 256)
            last = col >= 256
            key = jnp.where(last, 2 * WIN - 3 + row - 9 * part, row + WIN * (col >> 7))
            lane = jnp.where(last, end + THIRD * part, col & 127)
            got_heat = jnp.zeros((8, 128), f32)
            got_speed = jnp.zeros((8, 128), f32)
            for n in (*range(3, 29), *range(WIN + 3, WIN + 29), *range(2 * WIN, 2 * WIN + 9)):
                mine = key == n
                line_heat = jnp.broadcast_to(heat[n : n + 1, :], (8, 128))
                line_speed = jnp.broadcast_to(speed[n : n + 1, :], (8, 128))
                got_heat = jnp.where(mine, jnp.take_along_axis(line_heat, lane, axis=1), got_heat)
                got_speed = jnp.where(mine, jnp.take_along_axis(line_speed, lane, axis=1), got_speed)
            air_heat[pl.ds(start, 8), c * 128 : c * 128 + 128] = got_heat
            air_speed[pl.ds(start, 8), c * 128 : c * 128 + 128] = got_speed
        return carry

    lax.fori_loop(0, OROWS // 8, body, 0)
    for f, field in enumerate((air_heat, air_speed)):
        up[2 * f : 2 * f + 2, :] = field[OROWS - 2 : OROWS, :]
        down[2 * f : 2 * f + 2, :] = field[0:2, :]
    cross(place, up, down, x0, x1)


def ring_kernel(place, heat, speed, x0, x1, behind, east, west, before, after):
    cross(place, x1, x0, before, after)
    for out, col in ((east, 0), (west, OCOLS - 2)):
        out[0:OROWS, :] = jnp.concatenate([heat[:, col : col + 2], speed[:, col : col + 2]], axis=1)
        out[OROWS:WROWS, :] = jnp.zeros((WROWS - OROWS, 4), f32)
        for near, row in ((after, OROWS), (before, WROWS - 2)):
            out[row : row + 2, :] = jnp.concatenate([near[0:2, col : col + 2], near[2:4, col : col + 2]], axis=1)


def ocean_kernel(t, mask, heat, speed, before, after, east, west, air_before, air_after, air_east, air_west, out, win):
    gap = jnp.zeros((WROWS, 124), f32)
    strip = slice(STRIP_AT, STRIP_AT + WROWS)

    def window(field, slot, above, below, right, left):
        win[slot, OROWS:WROWS, :] = jnp.zeros((WROWS - OROWS, WCOLS), f32)
        win[slot, 0:OROWS, 0:OCOLS] = field
        for c in range(TILES):
            win[slot, OROWS : OROWS + 2, c * 128 : c * 128 + 128] = below(c)
            win[slot, WROWS - 2 : WROWS, c * 128 : c * 128 + 128] = above(c)
        win[slot, :, OCOLS:WCOLS] = jnp.concatenate([right, gap, left], axis=1)
        return win[slot]

    def sea_rows(wire):
        return lambda c: wire[SEA_AT + 2 * c : SEA_AT + 2 * c + 2, :]

    def level_rows(wire, l):
        return lambda c: wire[OCEAN_AT + 8 * c + 2 * l : OCEAN_AT + 8 * c + 2 * l + 2, :]

    def air_rows(wire, f):
        return lambda c: wire[2 * f : 2 * f + 2, c * 128 : c * 128 + 128]

    temps = [
        window(
            t[l], l, level_rows(before, l), level_rows(after, l),
            east[strip, 2 * l : 2 * l + 2], west[strip, 2 * l : 2 * l + 2],
        )
        for l in range(OLEV)
    ]
    sea = window(mask[...].astype(f32), 4, sea_rows(before), sea_rows(after), east[strip, 8:10], west[strip, 8:10])
    air = [
        window(
            field[...], 5 + f, air_rows(air_before, f), air_rows(air_after, f),
            air_east[:, 2 * f : 2 * f + 2], air_west[:, 2 * f : 2 * f + 2],
        )
        for f, field in enumerate((heat, speed))
    ]

    def beside(field):
        return (
            pltpu.roll(field, WCOLS - 1, 1),
            pltpu.roll(field, 1, 1),
            pltpu.roll(field, WROWS - 1, 0),
            pltpu.roll(field, 1, 0),
        )

    seas = beside(sea)
    rate = sea * flux_coef * air[1]
    for _ in range(2):
        temps[0] = temps[0] + rate * (air[0] - temps[0])
        moved = []
        for field in temps:
            total = jnp.zeros_like(field)
            for near_sea, near in zip(seas, beside(field)):
                total = total + near_sea * (near - field)
            moved.append(field + ocean_diffuse * (sea * total))
        temps = [
            moved[l]
            + vertical_mix * sea * (moved[max(l - 1, 0)] + moved[min(l + 1, OLEV - 1)] - 2.0 * moved[l])
            for l in range(OLEV)
        ]
    for l in range(OLEV):
        out[l, :, :] = temps[l][0:OROWS, 0:OCOLS]


def damp_window(lat_place, polar_rows, lat_total, band_rows):
    slots = np.arange(NLON)
    waves = np.where(slots < HALF, slots, np.where(slots == HALF, HALF, slots - HALF))
    weight = np.where((slots == 0) | (slots == HALF), 1.0, 2.0) / NLON
    sine = np.where(waves > 0, np.sin(np.pi * waves / NLON), 1.0)
    row_index = lat_place * ROWS - 4 + jnp.arange(WIN, dtype=jnp.int32)
    latitude_cos = jnp.sin(math.pi * (row_index.astype(f32) + 0.5) / lat_total)
    ratio = latitude_cos / math.sin(math.pi * band_rows / lat_total)
    damping = jnp.minimum(1.0, ratio[:, None] / sine.astype(np.float32)[None, :])
    damping = jnp.where(waves[None, :] > 0, damping, 1.0)
    listed = jnp.any(row_index[:, None] == polar_rows[None, :], axis=1)
    inside = (row_index >= 0) & (row_index < lat_total)
    table = jnp.where(listed[:, None], damping, 1.0) * weight.astype(np.float32)[None, :]
    return jnp.where(inside[:, None], table, 0.0)


def per_device(tracer, wind_u, wind_v, ocean_temp, land_mask, remap_rows, remap_cols, polar_rows):
    lat_devices = lax.axis_size("lat")
    lat_place, lon_place = lax.axis_index("lat"), lax.axis_index("lon")
    place = jnp.stack([lon_place, lat_place]).astype(jnp.int32)
    swaps = [
        [pair for i in range(start, lat_devices - 1, 2) for pair in ((i, i + 1), (i + 1, i))] for start in (1, 0)
    ]

    def along(x, s):
        return lax.ppermute(x, "lon", [(i, (i + s) % LONS) for i in range(LONS)])

    def across(first, second):
        got = lax.ppermute(first, "lat", swaps[0])
        return got, lax.ppermute(second, "lat", swaps[1])

    packed = call(
        pack_kernel,
        [sds(FIRST, 128)] * 4 + [sds(SECOND, 128)] * 4 + [sds(LAT_WIRE, 128)] * 2 + [sds(3, ROWS, COLS)],
        n_any=5,
        out_any=8,
        n_out=11,
        scratch=[pltpu.VMEM((LEV, ROWS, COLS), f32)] * 3
        + [
            pltpu.VMEM((OLEV, OROWS, OCOLS), f32),
            pltpu.VMEM((OROWS, OCOLS), jnp.int32),
            pltpu.VMEM((LAT_WIRE, 128), f32),
            pltpu.VMEM((LAT_WIRE, 128), f32),
            pltpu.VMEM((LONS, FIRST, 128), f32),
            pltpu.VMEM((LONS, SECOND, 128), f32),
            pltpu.SemaphoreType.DMA((4, LONS)),
            pltpu.SemaphoreType.DMA((2, LONS)),
        ],
        cost=cost(5),
        mib=60,
    )(tracer, wind_u, wind_v, ocean_temp, land_mask)
    mains, winds, mid = packed[:4], packed[4:8], packed[10]
    pieces = [mains[0]] + [along(mains[s], s) for s in (3, 2, 1)]
    near0, near1 = across(packed[8], packed[9])

    basis = call(basis_kernel, [sds(NLON, NLON, dtype=bf16)] * 2, n_in=4, cost=cost(3))(*wave_tables())
    damp = damp_window(lat_place, polar_rows, ROWS * lat_devices, lat_devices // 8 * ROWS)
    joined = call(
        join_kernel,
        [sds(RIM_WIRE if s in (1, 3) else STRIP_AT, 128) for s in range(LONS)]
        + [sds(WINDOW, 128)]
        + [sds(LAT_WIRE, 128)] * 2,
        smem=1,
        n_in=4,
        n_any=1,
        scratch=[pltpu.VMEM((WIN, 384), f32), pltpu.VMEM((3, ROWS, COLS), f32), pltpu.SemaphoreType.DMA],
        cost=cost(2),
    )(place, near0, near1, ocean_temp, land_mask, mid)
    before, after = joined[5:]
    windows = [joined[4]] + [along(joined[4], s) for s in (3, 2, 1)]
    rims = [joined[0]] + [along(joined[s], s) for s in (3, 2, 1)]
    blows = [winds[0]] + [along(winds[s], s) for s in (3, 2, 1)]

    heat, speed = call(bottom_kernel, [sds(TABLE, 128)] * 2, n_in=7, cost=cost(8))(*windows, damp, *basis)
    air_heat, air_speed, air_up, air_down = call(
        pick_kernel, [sds(OROWS, OCOLS)] * 2 + [sds(4, OCOLS)] * 2, smem=1, n_in=4, cost=cost(7),
        scratch=[pltpu.VMEM((4, OCOLS), f32)] * 2,
    )(place, remap_rows, remap_cols, heat, speed)
    air0, air1 = across(air_up, air_down)

    lines = (ROWS + 4) * LB
    far, top, rest = call(
        bulk_kernel,
        [sds(FT, 128)] + [sds(ROWS * LB, NLON, dtype=bf16)] * 2,
        n_in=15,
        n_any=1,
        scratch=[pltpu.VMEM((lines, NLON), f32)] + [pltpu.VMEM((lines - 16, NLON), f32)] * 3,
        cost=cost(13),
        mib=36,
    )(*pieces, *blows, *rims, damp, *basis, air_up)
    far = along(far, 2)
    one, three = call(finish_kernel, [sds(FT, 128)] * 2, n_in=4, cost=cost(2))(top, rest, *basis)
    own = call(own_kernel, sds(FT, 128), n_in=4, n_any=1, cost=cost(1))(top, rest, *basis, one)
    back = [own, along(one, 1), far, along(three, 3)]

    east, west, air_before, air_after = call(
        ring_kernel, [sds(WROWS, 4)] * 2 + [sds(4, OCOLS)] * 2, smem=1, n_in=4, n_any=1, cost=cost(1)
    )(place, air_heat, air_speed, air0, air1, top)
    air_east, air_west = along(east, LONS - 1), along(west, 1)
    ocean_out = call(
        ocean_kernel, sds(OLEV, OROWS, OCOLS), n_in=12, scratch=[pltpu.VMEM((7, WROWS, WCOLS), f32)], cost=cost(3)
    )(
        ocean_temp, land_mask, air_heat, air_speed, before, after, rims[1], rims[3],
        air_before, air_after, air_east, air_west,
    )
    scratch = [pltpu.VMEM((2, LB, ROWS, COLS), f32), pltpu.SemaphoreType.DMA((2,))]
    half = call(
        unpack_first, [sds(LEV, ROWS, COLS)], smem=1, n_in=2, out_any=1, n_out=1, scratch=scratch, cost=cost(1)
    )(place, back[0], back[2])[0]
    tracer_out = call(
        unpack_second, [sds(LEV, ROWS, COLS)], smem=1, n_in=2, n_any=1, out_any=1, n_out=1, scratch=scratch,
        cost=cost(1), aliases={3: 0},
    )(place, back[1], back[3], half)[0]
    return tracer_out, ocean_out


def solution(mesh):
    band = P(None, "lat", "lon")
    cells = P("lat", "lon")
    return jax.shard_map(
        per_device,
        mesh=mesh,
        in_specs=(band, band, band, band, cells, cells, cells, P()),
        out_specs=(band, band),
        check_vma=False,
    )
```
